32 devices in a mesh: ctx: 8 (over z, x), fsdp: 4 (over y, core).
Axes of the slice: x: 2, y: 2, z: 4, core: 2. Of those that a mesh axis runs over, the one named last changes fastest.
Arguments:
- inputs: bfloat16 [4, 1024, 1024], P('fsdp', 'ctx'), may hold values from -6 to 6
- segment_ids: int32 [4, 1024], P('fsdp', 'ctx'), may hold values from 0 to 1, never falling along the last dimension, each value on 1 to 768 neighbouring positions
- gain_attn: bfloat16 [1024], P(('ctx', 'fsdp')), may hold values from 0.5 to 1.5
- w_qkv: bfloat16 [1024, 3072], P(('ctx', 'fsdp')), may hold values from -4 to 4
- w_out_attn: bfloat16 [1024, 1024], P(('ctx', 'fsdp')), may hold values from -1.5 to 1.5
- gain_mlp: bfloat16 [1024], P(('ctx', 'fsdp')), may hold values from 0.5 to 1.5
- w_in: bfloat16 [1024, 5248], P(('ctx', 'fsdp')), may hold values from -0.1875 to 0.1875
- w_out_mlp: bfloat16 [2624, 1024], P(None, ('ctx', 'fsdp')), may hold values from -0.125 to 0.125
- cotangent: bfloat16 [4, 1024, 1024], P('fsdp', 'ctx'), may hold values from -6 to 6
Outputs:
- block_out: bfloat16 [4, 1024, 1024], P('fsdp', 'ctx')
- grad_input: bfloat16 [4, 1024, 1024], P('fsdp', 'ctx')
- grad_w_qkv: float32 [1024, 3072], P(('ctx', 'fsdp'))
- grad_w_out_attn: float32 [1024, 1024], P(('ctx', 'fsdp'))
- grad_w_in: float32 [1024, 5248], P(('ctx', 'fsdp'))
- grad_w_out_mlp: float32 [2624, 1024], P(None, ('ctx', 'fsdp'))
- grad_gain_attn: float32 [1024], P(('ctx', 'fsdp'))
- grad_gain_mlp: float32 [1024], P(('ctx', 'fsdp'))
The draws below stay inside these ranges and needn't reach their ends.
Inputs may be any that keep to these rules, and one draw needn't show every extreme that they name: `segment_ids`: along a row the ids never fall: segment 0 comes first, then segment 1; each segment holds 256 to 768 tokens.
All inputs are finite; a program needn't handle non-finite values.
Results may differ from the reference program's by a relative error of at most 0.015.
Values may be sent and summed in bfloat16 or wider, within the bound.
A program may use at most 256 MiB of HBM per device.

```python
import math
import jax
import jax.numpy as jnp
import numpy as np
from jax import lax

D = 1024
HEADS = 16
HD = 64
FF = 2624
SEQ_TOK = 1024
ROWS = 4
SEG_MOST = 768


def draw_w_qkv(key, part):
    base = jax.random.normal(key, (D, 3 * D), jnp.float32) * D ** (-0.5)
    return base.astype(jnp.bfloat16)


def steps_of(stream_key, dims, cuts, least, top_value):
    def one(position, shards_of):
        heights = jax.random.uniform(jax.random.fold_in(jax.random.fold_in(stream_key, 6), position), (shards_of,), jnp.float32, least / len(cuts), top_value / len(cuts))
        return jnp.repeat(jnp.exp(heights), dims[position] // shards_of).reshape((-1,) + (1,) * (len(dims) - position - 1))

    level = one(*cuts[0])
    for cut in cuts[1:]:
        level = level * one(*cut)
    return level


def profile(amount, total, limit, slope):
    weights = [(1 << 20) // math.isqrt(standing ** slope) + 1 for standing in range(2, amount + 1)]
    surplus, given = total - limit - (amount - 1), [1] * (amount - 1)
    while surplus > 0:
        candidates = [i for i in range(amount - 1) if given[i] < limit]
        pool, left = sum([weights[i] for i in candidates]), surplus
        for i in candidates:
            extra = min(limit - given[i], max(1, left * weights[i] // pool), surplus)
            given[i] = given[i] + extra
            surplus = surplus - extra
    return np.array([limit] + given)


def uneven_parts(own_key, count, total, reach, skew):
    if count == 2:
        one = jax.random.randint(own_key, (), max(1, total - reach), min(reach, total - 1) + 1)
        return jnp.stack([one, total - one])
    sizes = jnp.asarray(profile(count, total, reach, skew), jnp.int32)
    pairs = (count - 1) // 2
    giver, sink = sizes[1:1 + 2 * pairs:2], sizes[2:2 + 2 * pairs:2]
    slack = jnp.minimum(giver - 1, reach - sink)
    moved = jax.random.randint(jax.random.fold_in(own_key, 1), (pairs,), 0, 1 << 20) % (slack + 1)
    sizes = sizes.at[1:1 + 2 * pairs:2].set(giver - moved).at[2:2 + 2 * pairs:2].set(sink + moved)
    return sizes[jax.random.permutation(jax.random.fold_in(own_key, 2), count)]


def noise(stream_key, dims, deviation, most, cuts=(), held_as=jnp.bfloat16):
    result = jax.random.normal(stream_key, dims, jnp.float32) * deviation
    if len(cuts) > 0:
        result = steps_of(stream_key, dims, cuts, -0.22, 0.18) * result
    return jnp.clip(result, min=-most, max=most).astype(held_as)


def setup_inputs(seed: int = 0) -> dict:
    keys = jax.random.split(jax.random.key(seed), 10)
    return {
        "inputs": noise(keys[0], (ROWS, SEQ_TOK, D), 1.0, 6.0, ((0, 4), (1, 8))),
        "segment_ids": jax.vmap(lambda own: jnp.searchsorted(jnp.cumsum(uneven_parts(own, 2, SEQ_TOK, SEG_MOST, 0)), jnp.arange(SEQ_TOK), side="right"))(jax.random.split(keys[1], ROWS)).reshape((ROWS, SEQ_TOK)).astype(jnp.int32),
        "gain_attn": jnp.clip(1.0 + 0.1 * jax.random.normal(keys[2], (D,), jnp.float32), 0.5, 1.5).astype(jnp.bfloat16),
        "w_qkv": draw_w_qkv(jax.random.fold_in(keys[9], 71), 0),
        "w_out_attn": noise(keys[4], (D, D), (max(D * 16 // SEQ_TOK, 1)) ** -0.5, 1.5, ((0, 32),)),
        "gain_mlp": jnp.clip(1.0 + 0.1 * jax.random.normal(keys[5], (D,), jnp.float32), 0.5, 1.5).astype(jnp.bfloat16),
        "w_in": noise(keys[6], (D, 2 * FF), D ** -0.5, 0.1875, ((0, 32),)),
        "w_out_mlp": noise(keys[7], (FF, D), FF ** -0.5, 0.125, ((1, 32),)),
        "cotangent": noise(keys[8], (ROWS, SEQ_TOK, D), 1.0, 6.0, ((0, 4), (1, 8))),
    }


EPSILON = 1e-05
ROPE_BASE = 160000.0

def layer_norm(values):
    center = values - lax.optimization_barrier(jnp.mean(values, axis=-1, keepdims=True))
    scaled = lax.rsqrt(lax.optimization_barrier(jnp.mean(center * center, axis=-1, keepdims=True)) + EPSILON)
    return (center * scaled, scaled)

def norm_back(grad_norm, normed, scaled):
    return scaled * (grad_norm - lax.optimization_barrier(jnp.mean(grad_norm, axis=-1, keepdims=True)) - normed * lax.optimization_barrier(jnp.mean(grad_norm * normed, axis=-1, keepdims=True)))

def rope_tables(positions, head_size):
    freqs = ROPE_BASE ** (-jnp.arange(0, head_size, 2, dtype=jnp.float32) / head_size)
    angles = positions[:, None] * freqs[None, :]
    cosine = jnp.concatenate([jnp.cos(angles), jnp.cos(angles)], axis=-1)
    sine = jnp.concatenate([jnp.sin(angles), jnp.sin(angles)], axis=-1)
    return (cosine[:, None, :], sine[:, None, :])

def rotate(values, cosine, sine):
    half = values.shape[-1] // 2
    turned = jnp.concatenate([-values[..., half:], values[..., :half]], axis=-1)
    return values * cosine + turned * sine

def unrotate(grads, cosine, sine):
    half = grads.shape[-1] // 2
    weighted = grads * sine
    turned = jnp.concatenate([weighted[..., half:], -weighted[..., :half]], axis=-1)
    return grads * cosine + turned

def gelu_slope(values):
    return 0.5 * (1.0 + lax.erf(values * 0.7071067811865476)) + values * jnp.exp(-0.5 * values * values) * 0.3989422804014327

def reference(inputs, segment_ids, gain_attn, w_qkv, w_out_attn, gain_mlp, w_in, w_out_mlp, cotangent):
    scale = 1.0 / math.sqrt(HD)
    positions = jnp.arange(SEQ_TOK, dtype=jnp.int32).astype(jnp.float32)
    cosine, sine = rope_tables(positions, HD)
    gain_first = gain_attn.astype(jnp.float32)
    gain_second = gain_mlp.astype(jnp.float32)

    def one_row(carry, row):
        tokens_in, seg_row, grad_out = row
        tokens = tokens_in.astype(jnp.float32)
        same_doc = seg_row[:, None] == seg_row[None, :]
        normed_one, scale_one = layer_norm(tokens)
        normed_attn = (normed_one * gain_first).astype(jnp.bfloat16)
        projected = jnp.dot(normed_attn, w_qkv, preferred_element_type=jnp.float32)
        queries = rotate(projected[:, :D].reshape(SEQ_TOK, HEADS, HD), cosine, sine).astype(jnp.bfloat16)
        keys_rot = rotate(projected[:, D:2 * D].reshape(SEQ_TOK, HEADS, HD), cosine, sine).astype(jnp.bfloat16)
        values_all = projected[:, 2 * D:].astype(jnp.bfloat16).reshape(SEQ_TOK, HEADS, HD)
        query_heads = jnp.transpose(queries, (1, 0, 2))
        key_heads = jnp.transpose(keys_rot, (1, 0, 2))
        value_heads = jnp.transpose(values_all, (1, 0, 2))

        def head_scores(query_head, key_head):
            scores = jnp.dot(query_head, key_head.T, preferred_element_type=jnp.float32) * scale
            return jnp.where(same_doc, scores, -jnp.inf)

        def head_forward(pieces):
            query_head, key_head, value_head = pieces
            scores = head_scores(query_head, key_head)
            peak = lax.optimization_barrier(jnp.max(scores, axis=-1, keepdims=True))
            log_total = peak + jnp.log(lax.optimization_barrier(jnp.sum(jnp.exp(scores - peak), axis=-1, keepdims=True)))
            probs = jnp.exp(scores - log_total).astype(jnp.bfloat16)
            attended = jnp.dot(probs, value_head, preferred_element_type=jnp.float32).astype(jnp.bfloat16)
            return (attended, log_total)
        attended_heads, log_totals = lax.map(head_forward, (query_heads, key_heads, value_heads))
        attended = jnp.transpose(attended_heads, (1, 0, 2)).reshape(SEQ_TOK, D)
        residual = tokens + jnp.dot(attended, w_out_attn, preferred_element_type=jnp.float32)
        normed_two, scale_two = layer_norm(residual)
        normed_mlp = (normed_two * gain_second).astype(jnp.bfloat16)
        expanded = jnp.dot(normed_mlp, w_in, preferred_element_type=jnp.float32)
        pre_act = expanded[:, :FF]
        gate_part = expanded[:, FF:]
        activated = jax.nn.gelu(pre_act, approximate=False)
        product = (activated * gate_part).astype(jnp.bfloat16)
        block_out = (residual + jnp.dot(product, w_out_mlp, preferred_element_type=jnp.float32)).astype(jnp.bfloat16)
        grad_mlp_out = jnp.dot(product.T, grad_out, preferred_element_type=jnp.float32)
        grad_product = jnp.dot(grad_out, w_out_mlp.T, preferred_element_type=jnp.float32)
        grad_expanded = jnp.concatenate([grad_product * gate_part * gelu_slope(pre_act), grad_product * activated], axis=1).astype(jnp.bfloat16)
        grad_in_proj = jnp.dot(normed_mlp.T, grad_expanded, preferred_element_type=jnp.float32)
        grad_normed_mlp = jnp.dot(grad_expanded, w_in.T, preferred_element_type=jnp.float32)
        grad_gain_two = lax.optimization_barrier(jnp.sum(grad_normed_mlp * normed_two, axis=0))
        grad_residual = grad_out.astype(jnp.float32) + norm_back(grad_normed_mlp * gain_second, normed_two, scale_two)
        residual_half = grad_residual.astype(jnp.bfloat16)
        grad_out_proj = jnp.dot(attended.T, residual_half, preferred_element_type=jnp.float32)
        grad_attended = jnp.dot(residual_half, w_out_attn.T, preferred_element_type=jnp.float32).astype(jnp.bfloat16)
        grad_att_heads = jnp.transpose(grad_attended.reshape(SEQ_TOK, HEADS, HD), (1, 0, 2))

        def head_backward(pieces):
            query_head, key_head, value_head, grad_head, attended_head, log_total = pieces
            scores = head_scores(query_head, key_head)
            probs = jnp.exp(scores - log_total)
            probs_half = probs.astype(jnp.bfloat16)
            grad_probs = jnp.dot(grad_head, value_head.T, preferred_element_type=jnp.float32)
            row_dots = lax.optimization_barrier(jnp.sum(grad_head.astype(jnp.float32) * attended_head.astype(jnp.float32), axis=-1, keepdims=True))
            grad_scores = (probs * (grad_probs - row_dots)).astype(jnp.bfloat16)
            grad_query = jnp.dot(grad_scores, key_head, preferred_element_type=jnp.float32) * scale
            grad_key = jnp.dot(grad_scores.T, query_head, preferred_element_type=jnp.float32) * scale
            grad_value = jnp.dot(probs_half.T, grad_head, preferred_element_type=jnp.float32)
            return (grad_query, grad_key, grad_value)
        grad_q_heads, grad_k_heads, grad_v_heads = lax.map(head_backward, (query_heads, key_heads, value_heads, grad_att_heads, attended_heads, log_totals))
        grad_queries = unrotate(jnp.transpose(grad_q_heads, (1, 0, 2)), cosine, sine).reshape(SEQ_TOK, D)
        grad_keys = unrotate(jnp.transpose(grad_k_heads, (1, 0, 2)), cosine, sine).reshape(SEQ_TOK, D)
        grad_values = jnp.transpose(grad_v_heads, (1, 0, 2)).reshape(SEQ_TOK, D)
        grad_projected = jnp.concatenate([grad_queries, grad_keys, grad_values], axis=1).astype(jnp.bfloat16)
        grad_qkv = jnp.dot(normed_attn.T, grad_projected, preferred_element_type=jnp.float32)
        grad_normed_attn = jnp.dot(grad_projected, w_qkv.T, preferred_element_type=jnp.float32)
        grad_gain_one = lax.optimization_barrier(jnp.sum(grad_normed_attn * normed_one, axis=0))
        grad_tokens = (grad_residual + norm_back(grad_normed_attn * gain_first, normed_one, scale_one)).astype(jnp.bfloat16)
        totals = (carry[0] + grad_qkv, carry[1] + grad_out_proj, carry[2] + grad_in_proj, carry[3] + grad_mlp_out, carry[4] + grad_gain_one, carry[5] + grad_gain_two)
        return (totals, (block_out, grad_tokens))
    zeros = (jnp.zeros((D, 3 * D), jnp.float32), jnp.zeros((D, D), jnp.float32), jnp.zeros((D, 2 * FF), jnp.float32), jnp.zeros((FF, D), jnp.float32), jnp.zeros((D,), jnp.float32), jnp.zeros((D,), jnp.float32))
    totals, stacked = lax.scan(one_row, zeros, (inputs, segment_ids, cotangent))
    return (stacked[0], stacked[1], totals[0], totals[1], totals[2], totals[3], totals[4], totals[5])
```

```python
import functools
import math

import jax
import jax.numpy as jnp
from jax import lax
from jax.experimental import pallas as pl
from jax.experimental.pallas import tpu as pltpu
from jax.sharding import PartitionSpec as P

HEADS = 16
HD = 64


EPSILON = 1e-05
ROPE_BASE = 160000.0
MASKED = -1e30


def layer_norm(values):
    center = values - jnp.mean(values, axis=-1, keepdims=True)
    scaled = lax.rsqrt(jnp.mean(center * center, axis=-1, keepdims=True) + EPSILON)
    return (center * scaled, scaled)


def norm_back(grad_norm, normed, scaled):
    return scaled * (
        grad_norm
        - jnp.mean(grad_norm, axis=-1, keepdims=True)
        - normed * jnp.mean(grad_norm * normed, axis=-1, keepdims=True)
    )


def rope_columns(positions, head_size):
    freqs = ROPE_BASE ** (-jnp.arange(0, head_size, 2, dtype=jnp.float32) / head_size)
    angles = freqs[:, None] * positions[None, :]
    cosine = jnp.concatenate([jnp.cos(angles), jnp.cos(angles)], axis=0)
    sine = jnp.concatenate([jnp.sin(angles), jnp.sin(angles)], axis=0)
    return (cosine[None], sine[None])


def rotate_cols(values, cosine, sine):
    half = values.shape[1] // 2
    turned = jnp.concatenate([-values[:, half:], values[:, :half]], axis=1)
    return values * cosine + turned * sine


def unrotate_cols(grads, cosine, sine):
    half = grads.shape[1] // 2
    weighted = grads * sine
    turned = jnp.concatenate([weighted[:, half:], -weighted[:, :half]], axis=1)
    return grads * cosine + turned


def gelu_slope(values):
    return (
        0.5 * (1.0 + lax.erf(values * 0.7071067811865476))
        + values * jnp.exp(-0.5 * values * values) * 0.3989422804014327
    )


LANES = 128
QUERY_BLOCK = 256


def masked_scores(query, key, same, scale):
    scores = lax.dot_general(query, key, (((0,), (0,)), ((), ())), preferred_element_type=jnp.float32)
    return jnp.where(same, scores * scale, MASKED)


def attend_kernel(scale, query_ref, key_ref, value_ref, seg_own_ref, seg_ref, out_ref, log_ref):
    same = seg_own_ref[...] == seg_ref[...]
    scores = masked_scores(query_ref[0], key_ref[0], same, scale)
    peak = jnp.max(scores, axis=-1, keepdims=True)
    log_total = peak + jnp.log(jnp.sum(jnp.exp(scores - peak), axis=-1, keepdims=True))
    log_ref[0] = log_total
    probs = jnp.exp(scores - log_total).astype(jnp.bfloat16)
    out_ref[0] = lax.dot_general(
        value_ref[0], probs, (((1,), (1,)), ((), ())), preferred_element_type=jnp.float32
    ).astype(jnp.bfloat16)


def attend_grad_kernel(
    scale,
    query_ref,
    key_ref,
    value_ref,
    seg_own_ref,
    seg_ref,
    log_ref,
    grad_ref,
    attended_ref,
    query_grad_ref,
    key_grad_ref,
    value_grad_ref,
):
    @pl.when(pl.program_id(1) == 0)
    def _():
        key_grad_ref[...] = jnp.zeros_like(key_grad_ref)
        value_grad_ref[...] = jnp.zeros_like(value_grad_ref)

    query = query_ref[0]
    grad = grad_ref[0]
    key = key_ref[0]
    dots_row = jnp.sum(
        grad.astype(jnp.float32) * attended_ref[0].astype(jnp.float32), axis=0, keepdims=True
    )
    dots = jnp.transpose(jnp.broadcast_to(dots_row, (8, dots_row.shape[1])))[:, :1]
    same = seg_own_ref[...] == seg_ref[...]
    probs = jnp.exp(masked_scores(query, key, same, scale) - log_ref[0])
    grad_probs = lax.dot_general(
        grad, value_ref[0], (((0,), (0,)), ((), ())), preferred_element_type=jnp.float32
    )
    grad_scores = (probs * (grad_probs - dots)).astype(jnp.bfloat16)
    query_grad_ref[0] = scale * lax.dot_general(
        key, grad_scores, (((1,), (1,)), ((), ())), preferred_element_type=jnp.float32
    )
    key_grad_ref[0] += scale * lax.dot_general(
        query, grad_scores, (((1,), (0,)), ((), ())), preferred_element_type=jnp.float32
    )
    value_grad_ref[0] += lax.dot_general(
        grad, probs.astype(jnp.bfloat16), (((1,), (0,)), ((), ())), preferred_element_type=jnp.float32
    )


def attention_specs(head_size, row_count, block):
    part = pl.BlockSpec((1, head_size, block), lambda h, b: (h, 0, b))
    full = pl.BlockSpec((1, head_size, row_count), lambda h, b: (h, 0, 0))
    seg_own = pl.BlockSpec((block, 1), lambda h, b: (b, 0))
    seg_all = pl.BlockSpec((1, row_count), lambda h, b: (0, 0))
    log = pl.BlockSpec((1, block, 1), lambda h, b: (h, b, 0))
    return part, full, seg_own, seg_all, log


def attend(query_cols, key_cols, value_cols, seg_col, seg_row, scale):
    heads, head_size, row_count = query_cols.shape
    block = min(QUERY_BLOCK, row_count)
    part, full, own, every, log = attention_specs(head_size, row_count, block)
    return pl.pallas_call(
        lambda *refs: attend_kernel(scale, *refs),
        grid=(heads, row_count // block),
        in_specs=[part, full, full, own, every],
        out_specs=[part, log],
        out_shape=[
            jax.ShapeDtypeStruct((heads, head_size, row_count), jnp.bfloat16),
            jax.ShapeDtypeStruct((heads, row_count, 1), jnp.float32),
        ],
        name="attend",
    )(query_cols, key_cols, value_cols, seg_col, seg_row)


def attend_grads(
    query_cols, key_cols, value_cols, seg_col, seg_row, log_total, grad_cols, attended_cols, scale
):
    heads, head_size, row_count = query_cols.shape
    block = min(QUERY_BLOCK, row_count)
    part, full, own, every, log = attention_specs(head_size, row_count, block)
    grads = jax.ShapeDtypeStruct((heads, head_size, row_count), jnp.float32)
    return pl.pallas_call(
        lambda *refs: attend_grad_kernel(scale, *refs),
        grid=(heads, row_count // block),
        in_specs=[part, full, full, own, every, log, part, part],
        out_specs=[part, full, full],
        out_shape=[grads, grads, grads],
        name="attend_grads",
    )(query_cols, key_cols, value_cols, seg_col, seg_row, log_total, grad_cols, attended_cols)


MESH = pl.DeviceIdType.MESH


class Links:
    def __init__(self, ctx_size, fsdp_size, send_sems, recv_sems, local_sems):
        self.ctx_size = ctx_size
        self.fsdp_size = fsdp_size
        self.ctx = lax.axis_index("ctx")
        self.fsdp = lax.axis_index("fsdp")
        self.send_sems = send_sems
        self.recv_sems = recv_sems
        self.local_sems = local_sems
        self.used = 0
        self.used_local = 0

    def slot(self):
        self.used += 1
        return self.used - 1

    def ctx_copy(self, slot, src, dst, peer):
        return pltpu.make_async_remote_copy(
            src_ref=src,
            dst_ref=dst,
            send_sem=self.send_sems.at[slot],
            recv_sem=self.recv_sems.at[slot],
            device_id={"ctx": peer},
            device_id_type=MESH,
        )

    def fsdp_copy(self, slot, src, dst, peer):
        return pltpu.make_async_remote_copy(
            src_ref=src,
            dst_ref=dst,
            send_sem=self.send_sems.at[slot],
            recv_sem=self.recv_sems.at[slot],
            device_id={"fsdp": peer},
            device_id_type=MESH,
        )

    def local(self, src, dst):
        self.used_local += 1
        return pltpu.make_async_copy(src, dst, self.local_sems.at[self.used_local - 1])

    def barrier(self, over_ctx, over_fsdp):
        sem = pltpu.get_barrier_semaphore()
        count = 0
        if over_ctx:
            for k in range(1, self.ctx_size):
                pl.semaphore_signal(sem, inc=1, device_id={"ctx": self.ctx ^ k}, device_id_type=MESH)
                count += 1
        if over_fsdp:
            for k in range(1, self.fsdp_size):
                pl.semaphore_signal(sem, inc=1, device_id={"fsdp": self.fsdp ^ k}, device_id_type=MESH)
                count += 1
        pl.semaphore_wait(sem, count)


def run_tasks(tasks):
    live = list(tasks)
    while live:
        left = []
        for task in live:
            try:
                next(task)
                left.append(task)
            except StopIteration:
                pass
        live = left


def gather_ctx(links, own, place):
    c, n = links.ctx, links.ctx_size
    line = n // 2
    pos = c // 2
    pair_slots = {}
    right_slots = [None] + [links.slot() for s in range(1, line)]
    left_slots = [None] + [links.slot() for s in range(1, line)]
    own_slot = links.slot()
    from_left_slots = [None] + [links.slot() for s in range(1, line)]
    from_right_slots = [None] + [links.slot() for s in range(1, line)]

    def block(step):
        return (c + 2 * step + n) % n

    def right(step):
        source = own if step == 1 else place(block(1 - step))
        return links.ctx_copy(right_slots[step], source, place(block(1 - step)), (c + 2) % n)

    def left(step):
        source = own if step == 1 else place(block(step - 1))
        return links.ctx_copy(left_slots[step], source, place(block(step - 1)), (c + n - 2) % n)

    def pair(step):
        if step == 0:
            return links.ctx_copy(own_slot, own, place(c), c ^ 1)
        slot = from_left_slots[-step] if step < 0 else from_right_slots[step]
        return links.ctx_copy(slot, place(block(step)), place(block(step)), c ^ 1)

    def arrived_from_left(step):
        return links.ctx_copy(right_slots[step], own, place(block(-step)), c ^ 1)

    def arrived_from_right(step):
        return links.ctx_copy(left_slots[step], own, place(block(step)), c ^ 1)

    if line > 1:
        @pl.when(pos < line - 1)
        def _():
            right(1).start()

        @pl.when(pos > 0)
        def _():
            left(1).start()

    pair(0).start()
    yield
    for step in range(1, line):
        @pl.when(pos >= step)
        def _():
            arrived_from_left(step).wait_recv()
            if step < line - 1:
                @pl.when(pos < line - 1)
                def _():
                    right(step + 1).start()
            pair(-step).start()

        @pl.when(pos + step < line)
        def _():
            arrived_from_right(step).wait_recv()
            if step < line - 1:
                @pl.when(pos > 0)
                def _():
                    left(step + 1).start()
            pair(step).start()

        yield
    pair(0).wait_send()
    links.ctx_copy(own_slot, own, place(c ^ 1), c ^ 1).wait_recv()
    for step in range(1, line):
        @pl.when(pos < line - 1)
        def _():
            @pl.when(pos >= step - 1)
            def _():
                right(step).wait_send()

        @pl.when(pos > 0)
        def _():
            @pl.when(pos + step - 1 < line)
            def _():
                left(step).wait_send()

        @pl.when(pos >= step)
        def _():
            pair(-step).wait_send()
            links.ctx_copy(from_left_slots[step], own, place(block(-step) ^ 1), c ^ 1).wait_recv()

        @pl.when(pos + step < line)
        def _():
            pair(step).wait_send()
            links.ctx_copy(from_right_slots[step], own, place(block(step) ^ 1), c ^ 1).wait_recv()


def spread_ctx(links, source, place, arrived):
    copies = []
    for k in reversed(range(1, links.ctx_size)):
        peer = links.ctx ^ k
        slot = links.slot()
        links.ctx_copy(slot, source(peer), place(), peer).start()
        copies.append((slot, peer))
    yield
    for slot, peer in copies:
        links.ctx_copy(slot, source(peer), arrived(peer), peer).wait()


def spread_fsdp(links, source, place, arrived):
    copies = []
    for k in reversed(range(1, links.fsdp_size)):
        peer = links.fsdp ^ k
        slot = links.slot()
        links.fsdp_copy(slot, source(peer), place(), peer).start()
        copies.append((slot, peer))
    yield
    for slot, peer in copies:
        links.fsdp_copy(slot, source(peer), arrived(peer), peer).wait()


def gather_fsdp(links, own, place):
    f = links.fsdp
    far = []
    for k in range(2, links.fsdp_size, 2):
        slot = links.slot()
        links.fsdp_copy(slot, own, place(f), f ^ k).start()
        far.append((k, slot))
    near = links.slot()
    links.fsdp_copy(near, own, place(f), f ^ 1).start()
    yield
    passed = []
    for k, slot in far:
        links.fsdp_copy(slot, own, place(f ^ k), f ^ k).wait_recv()
        onward = links.slot()
        links.fsdp_copy(onward, place(f ^ k), place(f ^ k), f ^ 1).start()
        passed.append((k, onward))
    yield
    links.fsdp_copy(near, own, place(f ^ 1), f ^ 1).wait()
    for k, slot in far:
        links.fsdp_copy(slot, own, place(f), f ^ k).wait_send()
    for k, onward in passed:
        links.fsdp_copy(onward, place(f ^ k), place(f ^ 1 ^ k), f ^ 1).wait()


def local_task(links, pairs):
    copies = [links.local(src, dst) for src, dst in pairs]
    for copy in copies:
        copy.start()
    yield
    yield
    yield
    for copy in copies:
        copy.wait()


def after(first, second):
    yield from first
    yield from second()


def exchange(name, number, sizes, make_tasks, operands, outs, over_ctx=True, over_fsdp=True, slots=96):
    ctx_size, fsdp_size = sizes

    def kernel(*refs):
        ins = refs[: len(operands)]
        results = refs[len(operands) : len(operands) + len(outs)]
        send_sems, recv_sems, local_sems = refs[len(operands) + len(outs) :]
        links = Links(ctx_size, fsdp_size, send_sems, recv_sems, local_sems)
        links.barrier(over_ctx, over_fsdp)
        run_tasks(make_tasks(links, ins, results))

    anywhere = pl.BlockSpec(memory_space=pl.ANY)
    return pl.pallas_call(
        kernel,
        in_specs=[anywhere] * len(operands),
        out_specs=[anywhere] * len(outs),
        out_shape=[jax.ShapeDtypeStruct(shape, dtype) for shape, dtype in outs],
        scratch_shapes=[
            pltpu.SemaphoreType.DMA((slots,)),
            pltpu.SemaphoreType.DMA((slots,)),
            pltpu.SemaphoreType.DMA((16,)),
        ],
        compiler_params=pltpu.CompilerParams(collective_id=number, has_side_effects=True),
        name=name,
    )(*operands)


def gather_all(sizes, tokens, seg, qkv_parts, out_rows, in_parts, mlp_parts, grad_out):
    n, fs = sizes
    bf16 = jnp.bfloat16

    def tasks(links, ins, outs):
        tokens_ref, seg_ref, qkv_ref, out_ref, in_ref, mlp_ref, grad_ref = ins
        tokens_all, seg_all, qkv_all, out_all, in_all, mlp_all, grad_all = outs
        c, f = links.ctx, links.fsdp
        chip, core = f // 2, f % 2
        staged = [
            (qkv_ref.at[c], qkv_all.at[c, f]),
            (out_ref, out_all.at[c, chip, core]),
            (in_ref.at[f], in_all.at[c, f]),
            (mlp_ref.at[f], mlp_all.at[c, f]),
        ]
        copies = [links.local(src, dst) for src, dst in staged]
        for copy in copies:
            copy.start()

        def weights(source_ref, all_ref, copy):
            def spread():
                yield from spread_fsdp(
                    links,
                    lambda peer: source_ref.at[peer],
                    lambda: all_ref.at[c, f],
                    lambda peer: all_ref.at[c, peer],
                )
                copy.wait()
                yield from gather_ctx(links, all_ref.at[c], lambda b: all_ref.at[b])
            return spread()

        def qkv():
            yield from spread_ctx(
                links,
                lambda peer: qkv_ref.at[peer],
                lambda: qkv_all.at[c, f],
                lambda peer: qkv_all.at[peer, f],
            )
            copies[0].wait()
            yield from gather_fsdp(links, qkv_all.at[:, f], lambda b: qkv_all.at[:, b])

        def out_weights():
            far = []
            for k in range(2, fs, 2):
                slot = links.slot()
                links.fsdp_copy(slot, out_ref, out_all.at[c, chip, core], f ^ k).start()
                far.append((slot, k))
            yield
            for slot, k in far:
                links.fsdp_copy(slot, out_ref, out_all.at[c, (f ^ k) // 2, core], f ^ k).wait()
            copies[1].wait()
            yield from gather_ctx(links, out_all.at[c, :, core], lambda b: out_all.at[b, :, core])
            slot = links.slot()
            links.fsdp_copy(slot, out_all.at[:, :, core], out_all.at[:, :, core], f ^ 1).start()
            yield
            links.fsdp_copy(slot, out_all.at[:, :, core], out_all.at[:, :, 1 - core], f ^ 1).wait()

        return [
            qkv(),
            gather_ctx(links, tokens_ref, lambda b: tokens_all.at[b]),
            spread_ctx(links, lambda peer: seg_ref, lambda: seg_all.at[c], lambda peer: seg_all.at[peer]),
            out_weights(),
            weights(in_ref, in_all, copies[2]),
            weights(mlp_ref, mlp_all, copies[3]),
            gather_fsdp(links, grad_ref, lambda b: grad_all.at[b]),
            local_task(
                links,
                [(tokens_ref, tokens_all.at[c]), (seg_ref, seg_all.at[c]), (grad_ref, grad_all.at[f])],
            ),
        ]

    outs = [
        ((n,) + tokens.shape, bf16),
        ((n,) + seg.shape, seg.dtype),
        ((n, fs) + qkv_parts.shape[1:], bf16),
        ((n, fs // 2, 2) + out_rows.shape, bf16),
        ((n, fs) + in_parts.shape[1:], bf16),
        ((n, fs) + mlp_parts.shape[1:], bf16),
        ((fs,) + grad_out.shape, bf16),
    ]
    return exchange(
        "gather_all",
        1,
        sizes,
        tasks,
        (tokens, seg, qkv_parts, out_rows, in_parts, mlp_parts, grad_out),
        outs,
        slots=12 * (n + fs),
    )


def swap_task(links, axis, src, out):
    me = links.ctx if axis == "ctx" else links.fsdp
    spread = spread_ctx if axis == "ctx" else spread_fsdp
    yield from spread(links, lambda peer: src.at[peer], lambda: out.at[me], lambda peer: out.at[peer])


def swaps(name, number, sizes, axes, arrays):
    def tasks(links, ins, outs):
        result = []
        own = []
        for axis, src, out in zip(axes, ins, outs):
            me = links.ctx if axis == "ctx" else links.fsdp
            if axis == "gather":
                result.append(gather_fsdp(links, src, lambda b, out=out: out.at[b]))
                own.append((src, out.at[me]))
            else:
                result.append(swap_task(links, axis, src, out))
                own.append((src.at[me], out.at[me]))
        return result + [local_task(links, own)]

    outs = [
        (((sizes[1],) if axis == "gather" else ()) + array.shape, array.dtype)
        for axis, array in zip(axes, arrays)
    ]
    return exchange(
        name,
        number,
        sizes,
        tasks,
        tuple(arrays),
        outs,
        over_ctx="ctx" in axes,
        over_fsdp="fsdp" in axes or "gather" in axes,
        slots=4 * (sizes[0] + sizes[1]),
    )


def pair_stage(number, sizes, halves, fsdp_arrays):
    n, fs = sizes

    def tasks(links, ins, outs):
        c = links.ctx
        result = []
        for src, out in zip(ins[: len(halves)], outs):
            def send(src=src, out=out):
                slots = []
                for q in range(n // 2):
                    slot = links.slot()
                    slots.append(slot)
                    links.ctx_copy(slot, src.at[q, 1 - c % 2], out.at[q], c ^ 1).start()
                yield
                for q, slot in enumerate(slots):
                    links.ctx_copy(slot, src.at[q, 1 - c % 2], out.at[q], c ^ 1).wait()
            result.append(send())
        own = []
        for src, out in zip(ins[len(halves) :], outs[len(halves) :]):
            result.append(swap_task(links, "fsdp", src, out))
            own.append((src.at[links.fsdp], out.at[links.fsdp]))
        return result + [local_task(links, own)]

    outs = [((array.shape[0],) + array.shape[2:], array.dtype) for array in halves]
    outs += [(array.shape, array.dtype) for array in fsdp_arrays]
    return exchange("pair_stage", number, sizes, tasks, tuple(halves) + tuple(fsdp_arrays), outs)


def line_stage(number, sizes, lines, ctx_arrays):
    n, fs = sizes

    def tasks(links, ins, outs):
        c = links.ctx
        pos = c // 2
        result = []
        own = []
        for src, out in zip(ins[: len(lines)], outs):
            own.append((src.at[pos], out.at[pos]))
            def send(src=src, out=out):
                slots = []
                for k in reversed(range(1, n // 2)):
                    slot = links.slot()
                    slots.append((slot, k))
                    links.ctx_copy(slot, src.at[pos ^ k], out.at[pos], c ^ (2 * k)).start()
                yield
                for slot, k in slots:
                    links.ctx_copy(slot, src.at[pos ^ k], out.at[pos ^ k], c ^ (2 * k)).wait()
            result.append(send())
        for src, out in zip(ins[len(lines) :], outs[len(lines) :]):
            result.append(swap_task(links, "ctx", src, out))
            own.append((src.at[c], out.at[c]))
        return result + [local_task(links, own)]

    outs = [(array.shape, array.dtype) for array in tuple(lines) + tuple(ctx_arrays)]
    return exchange(
        "line_stage", number, sizes, tasks, tuple(lines) + tuple(ctx_arrays), outs, over_fsdp=False
    )


def pick(array, index, axis):
    return lax.dynamic_index_in_dim(array, index, axis, keepdims=False)


def body(
    ctx_size,
    fsdp_size,
    inputs,
    segment_ids,
    gain_attn,
    w_qkv,
    w_out_attn,
    gain_mlp,
    w_in,
    w_out_mlp,
    cotangent,
):
    tok_count, width = inputs.shape[1:]
    heads = HEADS
    head_size = HD
    scale = 1.0 / math.sqrt(head_size)
    hidden_units = w_out_mlp.shape[0]
    row_count = ctx_size * tok_count
    own_heads = heads // ctx_size
    own_width = own_heads * head_size
    weight_rows = w_qkv.shape[0]
    own_hidden = hidden_units // fsdp_size
    own_out = width // fsdp_size
    line = ctx_size // 2
    block_rows = width // ctx_size
    sizes = (ctx_size, fsdp_size)
    bf16 = jnp.bfloat16
    f32 = jnp.float32
    ctx_index = lax.axis_index("ctx")
    parity = ctx_index % 2
    pos = ctx_index // 2

    qkv_parts = jnp.transpose(
        w_qkv.reshape(weight_rows, 3, ctx_size, own_width), (2, 0, 1, 3)
    ).reshape(ctx_size, weight_rows, 3 * own_width)
    gains_own = jnp.pad(jnp.stack([gain_attn, gain_mlp], axis=1), ((0, 0), (0, LANES - 2)))
    qkv_parts = jnp.concatenate(
        [qkv_parts, jnp.broadcast_to(gains_own, (ctx_size, weight_rows, LANES))], axis=2
    )
    in_parts = jnp.transpose(
        w_in.reshape(weight_rows, 2, fsdp_size, own_hidden), (2, 0, 1, 3)
    ).reshape(fsdp_size, weight_rows, 2 * own_hidden)
    mlp_parts = jnp.transpose(w_out_mlp.reshape(fsdp_size, own_hidden, weight_rows), (0, 2, 1))
    seg_own = jnp.broadcast_to(segment_ids.astype(f32), (8, tok_count))

    tokens_all, seg_all, qkv_all, out_all, in_all, mlp_all, grad_out_group = gather_all(
        sizes, inputs[0], seg_own, qkv_parts, w_out_attn, in_parts, mlp_parts, cotangent[0]
    )
    qkv_got = qkv_all.reshape(width, 3 * own_width + LANES)
    qkv_mine = qkv_got[:, : 3 * own_width]
    gains = qkv_got[:, 3 * own_width : 3 * own_width + 2].astype(f32).T
    gain_first = gains[0]
    gain_second = gains[1]
    attn_full = out_all.reshape(width, width)
    in_mine = in_all.reshape(width, 2 * own_hidden)
    mlp_turned = mlp_all.reshape(width, own_hidden)

    seg_row = seg_all[:, 0].reshape(1, row_count)
    seg_col = seg_row.reshape(row_count, 1)
    row_tokens = tokens_all.reshape(row_count, width).astype(f32)
    row_normed, unused = layer_norm(row_tokens)
    row_normed_attn = (row_normed * gain_first).astype(bf16)
    tokens = inputs[0].astype(f32)
    normed_one, scale_one = layer_norm(tokens)

    projected_cols = jnp.einsum(
        "de,td->et", qkv_mine, row_normed_attn, preferred_element_type=f32
    ).reshape(3, own_heads, head_size, row_count)
    positions = jnp.arange(row_count, dtype=jnp.int32).astype(f32)
    cosine, sine = rope_columns(positions, head_size)
    query_cols = rotate_cols(projected_cols[0], cosine, sine).astype(bf16)
    key_cols = rotate_cols(projected_cols[1], cosine, sine).astype(bf16)
    value_cols = projected_cols[2].astype(bf16)
    row_attended, log_total = attend(query_cols, key_cols, value_cols, seg_col, seg_row, scale)

    (attended,) = swaps(
        "swap_attended",
        2,
        sizes,
        ("ctx",),
        (row_attended.reshape(own_width, row_count).T.reshape(ctx_size, tok_count, own_width),),
    )
    attended = jnp.transpose(attended, (1, 0, 2)).reshape(tok_count, width)
    residual = tokens + jnp.dot(attended, attn_full, preferred_element_type=f32)
    normed_two, scale_two = layer_norm(residual)
    normed_mlp = (normed_two * gain_second).astype(bf16)
    (normed_group,) = swaps("gather_normed", 3, sizes, ("gather",), (normed_mlp,))
    group = fsdp_size * tok_count
    normed_group = normed_group.reshape(group, width)
    grad_out_group = grad_out_group.reshape(group, width)

    expanded = jnp.dot(normed_group, in_mine, preferred_element_type=f32)
    pre_act = expanded[:, :own_hidden]
    gate_part = expanded[:, own_hidden:]
    activated = jax.nn.gelu(pre_act, approximate=False)
    product = (activated * gate_part).astype(bf16)
    grad_product = jnp.einsum("td,df->tf", grad_out_group, mlp_turned, preferred_element_type=f32)
    grad_expanded = jnp.concatenate(
        [grad_product * gate_part * gelu_slope(pre_act), grad_product * activated], axis=1
    ).astype(bf16)
    grad_normed_part = jnp.einsum(
        "tf,df->td", grad_expanded, in_mine, preferred_element_type=f32
    ).astype(bf16)
    out_part = jnp.einsum("tf,df->td", product, mlp_turned, preferred_element_type=f32).astype(bf16)

    (grad_normed_parts,) = swaps(
        "swap_grad_normed",
        4,
        sizes,
        ("fsdp",),
        (grad_normed_part.reshape(fsdp_size, tok_count, width),),
    )
    grad_normed_mlp = jnp.sum(grad_normed_parts.astype(f32), axis=0)

    normed_halves = normed_group.reshape(group, line, 2, block_rows)
    grad_out_halves = grad_out_group.reshape(group, line, 2, block_rows)

    def mlp_grads(side):
        left = pick(normed_halves, side, 2).reshape(group, line * block_rows)
        right = pick(grad_out_halves, side, 2).reshape(group, line * block_rows)
        grad_in = jnp.einsum("td,tf->df", left, grad_expanded, preferred_element_type=f32)
        grad_mlp = jnp.einsum("td,tf->df", right, product, preferred_element_type=f32)
        return grad_in, grad_mlp

    swap_pair = [(i, i ^ 1) for i in range(ctx_size)]
    other_in, other_mlp = mlp_grads(1 - parity)
    other_in = lax.ppermute(other_in.astype(bf16), "ctx", swap_pair)
    other_mlp = lax.ppermute(other_mlp.astype(bf16), "ctx", swap_pair)
    mine_in, mine_mlp = mlp_grads(parity)
    sum_in = (mine_in + other_in.astype(f32)).reshape(line, block_rows, 2 * own_hidden)
    sum_mlp = (mine_mlp + other_mlp.astype(f32)).reshape(line, block_rows, own_hidden)

    def line_sum(blocks):
        total = pick(blocks, pos, 0)
        half = blocks.astype(bf16)
        for k in reversed(range(1, line)):
            moved = lax.ppermute(
                pick(half, pos ^ k, 0), "ctx", [(i, i ^ (2 * k)) for i in range(ctx_size)]
            )
            total = total + moved.astype(f32)
        return total.astype(bf16)

    grad_in_block = line_sum(sum_in)
    grad_mlp_block = line_sum(sum_mlp)

    grad_gain_two = jnp.sum(grad_normed_mlp * normed_two, axis=0)
    grad_residual = cotangent[0].astype(f32) + norm_back(
        grad_normed_mlp * gain_second, normed_two, scale_two
    )
    residual_half = grad_residual.astype(bf16)
    grad_attended = jnp.einsum(
        "te,de->td", residual_half, attn_full, preferred_element_type=f32
    ).astype(bf16)
    row_grad, residual_cols, attended_group = swaps(
        "swap_grad_attended",
        5,
        sizes,
        ("ctx", "fsdp", "gather"),
        (
            jnp.transpose(grad_attended.reshape(tok_count, ctx_size, own_width), (1, 0, 2)),
            jnp.transpose(residual_half.reshape(tok_count, fsdp_size, own_out), (1, 0, 2)),
            attended,
        ),
    )
    grad_attn_part = jnp.einsum(
        "td,te->de",
        attended_group.reshape(group, width),
        residual_cols.reshape(group, own_out),
        preferred_element_type=f32,
    ).reshape(line, 2, block_rows, own_out)
    row_grad_cols = row_grad.reshape(row_count, own_width).T.reshape(
        own_heads, head_size, row_count
    )
    grad_query, grad_key, grad_value = attend_grads(
        query_cols,
        key_cols,
        value_cols,
        seg_col,
        seg_row,
        log_total,
        row_grad_cols,
        row_attended,
        scale,
    )
    grad_proj_cols = (
        jnp.stack(
            [
                unrotate_cols(grad_query, cosine, sine),
                unrotate_cols(grad_key, cosine, sine),
                grad_value,
            ],
            axis=0,
        )
        .astype(bf16)
        .reshape(3 * own_width, row_count)
    )
    row_grad_normed = jnp.einsum("de,et->td", qkv_mine, grad_proj_cols, preferred_element_type=f32)
    grad_gain_part = jnp.sum(row_grad_normed * row_normed, axis=0)
    gain_columns = jnp.pad(
        jnp.stack([grad_gain_part, grad_gain_two], axis=1), ((0, 0), (0, LANES - 2))
    )
    qkv_terms = jnp.concatenate(
        [
            jnp.einsum("td,et->de", row_normed_attn, grad_proj_cols, preferred_element_type=f32),
            gain_columns,
        ],
        axis=1,
    ).astype(bf16)
    qkv_width = 3 * own_width + LANES
    qkv_terms = jnp.transpose(
        qkv_terms.reshape(ctx_size, fsdp_size, weight_rows, qkv_width), (1, 0, 2, 3)
    )
    row_grad_blocks = row_grad_normed.reshape(line, 2, tok_count, width)
    row_grad_half = row_grad_blocks.astype(bf16)
    grad_attn_half = grad_attn_part.astype(bf16)
    row_other, attn_other, qkv_got_terms, out_parts = pair_stage(
        6,
        sizes,
        (row_grad_half, grad_attn_half),
        (qkv_terms, out_part.reshape(fsdp_size, tok_count, width)),
    )
    block_out = (residual + jnp.sum(out_parts.astype(f32), axis=0)).astype(bf16)
    row_sum = (pick(row_grad_half, parity, 1).astype(f32) + row_other.astype(f32)).astype(bf16)
    attn_sum = (pick(grad_attn_half, parity, 1).astype(f32) + attn_other.astype(f32)).astype(bf16)
    qkv_half = jnp.sum(qkv_got_terms.astype(f32), axis=0).astype(bf16)
    row_lines, attn_lines, qkv_lines = line_stage(7, sizes, (row_sum, attn_sum), (qkv_half,))
    grad_normed_attn = jnp.sum(row_lines.astype(f32), axis=0)
    grad_attn_block = jnp.sum(attn_lines.astype(f32), axis=0).astype(bf16)
    grad_tokens = (
        grad_residual + norm_back(grad_normed_attn * gain_first, normed_one, scale_one)
    ).astype(bf16)
    grad_qkv_rows = jnp.transpose(
        qkv_lines[:, :, : 3 * own_width].astype(f32).reshape(ctx_size, weight_rows, 3, own_width),
        (1, 2, 0, 3),
    ).reshape(weight_rows, 3 * width)
    gain_sums = jnp.sum(qkv_lines[:, :, 3 * own_width : 3 * own_width + 2].astype(f32), axis=0)

    in_got, mlp_got, attn_got = swaps(
        "swap_weight_grads",
        8,
        sizes,
        ("fsdp", "fsdp", "fsdp"),
        (
            grad_in_block.reshape(fsdp_size, weight_rows, 2 * own_hidden),
            grad_mlp_block.reshape(fsdp_size, weight_rows, own_hidden),
            grad_attn_block.reshape(fsdp_size, weight_rows, own_out),
        ),
    )
    grad_in_rows = jnp.transpose(
        in_got.astype(f32).reshape(fsdp_size, weight_rows, 2, own_hidden), (1, 2, 0, 3)
    ).reshape(weight_rows, 2 * hidden_units)
    grad_mlp_cols = jnp.transpose(mlp_got.astype(f32), (0, 2, 1)).reshape(hidden_units, weight_rows)
    grad_attn_rows = jnp.transpose(attn_got.astype(f32), (1, 0, 2)).reshape(weight_rows, width)
    return (
        block_out[None],
        grad_tokens[None],
        grad_qkv_rows,
        grad_attn_rows,
        grad_in_rows,
        grad_mlp_cols,
        gain_sums[:, 0],
        gain_sums[:, 1],
    )


def solution(mesh):
    in_specs = (
        P("fsdp", "ctx", None),
        P("fsdp", "ctx"),
        P(("ctx", "fsdp")),
        P(("ctx", "fsdp"), None),
        P(("ctx", "fsdp"), None),
        P(("ctx", "fsdp")),
        P(("ctx", "fsdp"), None),
        P(None, ("ctx", "fsdp")),
        P("fsdp", "ctx", None),
    )
    out_specs = (
        P("fsdp", "ctx", None),
        P("fsdp", "ctx", None),
        P(("ctx", "fsdp"), None),
        P(("ctx", "fsdp"), None),
        P(("ctx", "fsdp"), None),
        P(None, ("ctx", "fsdp")),
        P(("ctx", "fsdp")),
        P(("ctx", "fsdp")),
    )
    step = functools.partial(body, mesh.shape["ctx"], mesh.shape["fsdp"])
    return jax.shard_map(step, mesh=mesh, in_specs=in_specs, out_specs=out_specs, check_vma=False)
```

```python
import functools
import math

import jax
import jax.numpy as jnp
from jax import lax
from jax.experimental import pallas as pl
from jax.experimental.pallas import tpu as pltpu
from jax.sharding import PartitionSpec as P

HEADS = 16
HD = 64


EPSILON = 1e-05
ROPE_BASE = 160000.0
MASKED = -1e30


def layer_norm(values):
    center = values - jnp.mean(values, axis=-1, keepdims=True)
    scaled = lax.rsqrt(jnp.mean(center * center, axis=-1, keepdims=True) + EPSILON)
    return (center * scaled, scaled)


def norm_back(grad_norm, normed, scaled):
    return scaled * (
        grad_norm
        - jnp.mean(grad_norm, axis=-1, keepdims=True)
        - normed * jnp.mean(grad_norm * normed, axis=-1, keepdims=True)
    )


def rope_columns(positions, head_size):
    freqs = ROPE_BASE ** (-jnp.arange(0, head_size, 2, dtype=jnp.float32) / head_size)
    angles = freqs[:, None] * positions[None, :]
    cosine = jnp.concatenate([jnp.cos(angles), jnp.cos(angles)], axis=0)
    sine = jnp.concatenate([jnp.sin(angles), jnp.sin(angles)], axis=0)
    return (cosine[None], sine[None])


def rotate_cols(values, cosine, sine):
    half = values.shape[1] // 2
    turned = jnp.concatenate([-values[:, half:], values[:, :half]], axis=1)
    return values * cosine + turned * sine


def unrotate_cols(grads, cosine, sine):
    half = grads.shape[1] // 2
    weighted = grads * sine
    turned = jnp.concatenate([weighted[:, half:], -weighted[:, :half]], axis=1)
    return grads * cosine + turned


def gelu_slope(values):
    return (
        0.5 * (1.0 + lax.erf(values * 0.7071067811865476))
        + values * jnp.exp(-0.5 * values * values) * 0.3989422804014327
    )


LANES = 128
QUERY_BLOCK = 256


def masked_scores(query, key, same, scale):
    scores = lax.dot_general(query, key, (((0,), (0,)), ((), ())), preferred_element_type=jnp.float32)
    return jnp.where(same, scores * scale, MASKED)


def attend_kernel(scale, query_ref, key_ref, value_ref, seg_own_ref, seg_ref, out_ref, log_ref):
    same = seg_own_ref[...] == seg_ref[...]
    scores = masked_scores(query_ref[0], key_ref[0], same, scale)
    peak = jnp.max(scores, axis=-1, keepdims=True)
    log_total = peak + jnp.log(jnp.sum(jnp.exp(scores - peak), axis=-1, keepdims=True))
    log_ref[0] = log_total
    probs = jnp.exp(scores - log_total).astype(jnp.bfloat16)
    out_ref[0] = lax.dot_general(
        value_ref[0], probs, (((1,), (1,)), ((), ())), preferred_element_type=jnp.float32
    ).astype(jnp.bfloat16)


def attend_grad_kernel(
    scale,
    query_ref,
    key_ref,
    value_ref,
    seg_own_ref,
    seg_ref,
    log_ref,
    grad_ref,
    attended_ref,
    query_grad_ref,
    key_grad_ref,
    value_grad_ref,
):
    @pl.when(pl.program_id(1) == 0)
    def _():
        key_grad_ref[...] = jnp.zeros_like(key_grad_ref)
        value_grad_ref[...] = jnp.zeros_like(value_grad_ref)

    query = query_ref[0]
    grad = grad_ref[0]
    key = key_ref[0]
    dots_row = jnp.sum(
        grad.astype(jnp.float32) * attended_ref[0].astype(jnp.float32), axis=0, keepdims=True
    )
    dots = jnp.transpose(jnp.broadcast_to(dots_row, (8, dots_row.shape[1])))[:, :1]
    same = seg_own_ref[...] == seg_ref[...]
    probs = jnp.exp(masked_scores(query, key, same, scale) - log_ref[0])
    grad_probs = lax.dot_general(
        grad, value_ref[0], (((0,), (0,)), ((), ())), preferred_element_type=jnp.float32
    )
    grad_scores = (probs * (grad_probs - dots)).astype(jnp.bfloat16)
    query_grad_ref[0] = scale * lax.dot_general(
        key, grad_scores, (((1,), (1,)), ((), ())), preferred_element_type=jnp.float32
    )
    key_grad_ref[0] += scale * lax.dot_general(
        query, grad_scores, (((1,), (0,)), ((), ())), preferred_element_type=jnp.float32
    )
    value_grad_ref[0] += lax.dot_general(
        grad, probs.astype(jnp.bfloat16), (((1,), (0,)), ((), ())), preferred_element_type=jnp.float32
    )


def attention_specs(head_size, row_count, block):
    part = pl.BlockSpec((1, head_size, block), lambda h, b: (h, 0, b))
    full = pl.BlockSpec((1, head_size, row_count), lambda h, b: (h, 0, 0))
    seg_own = pl.BlockSpec((block, 1), lambda h, b: (b, 0))
    seg_all = pl.BlockSpec((1, row_count), lambda h, b: (0, 0))
    log = pl.BlockSpec((1, block, 1), lambda h, b: (h, b, 0))
    return part, full, seg_own, seg_all, log


def attend(query_cols, key_cols, value_cols, seg_col, seg_row, scale):
    heads, head_size, row_count = query_cols.shape
    block = min(QUERY_BLOCK, row_count)
    part, full, own, every, log = attention_specs(head_size, row_count, block)
    return pl.pallas_call(
        lambda *refs: attend_kernel(scale, *refs),
        grid=(heads, row_count // block),
        in_specs=[part, full, full, own, every],
        out_specs=[part, log],
        out_shape=[
            jax.ShapeDtypeStruct((heads, head_size, row_count), jnp.bfloat16),
            jax.ShapeDtypeStruct((heads, row_count, 1), jnp.float32),
        ],
        name="attend",
    )(query_cols, key_cols, value_cols, seg_col, seg_row)


def attend_grads(
    query_cols, key_cols, value_cols, seg_col, seg_row, log_total, grad_cols, attended_cols, scale
):
    heads, head_size, row_count = query_cols.shape
    block = min(QUERY_BLOCK, row_count)
    part, full, own, every, log = attention_specs(head_size, row_count, block)
    grads = jax.ShapeDtypeStruct((heads, head_size, row_count), jnp.float32)
    return pl.pallas_call(
        lambda *refs: attend_grad_kernel(scale, *refs),
        grid=(heads, row_count // block),
        in_specs=[part, full, full, own, every, log, part, part],
        out_specs=[part, full, full],
        out_shape=[grads, grads, grads],
        name="attend_grads",
    )(query_cols, key_cols, value_cols, seg_col, seg_row, log_total, grad_cols, attended_cols)


MESH = pl.DeviceIdType.MESH


class Links:
    def __init__(self, ctx_size, fsdp_size, send_sems, recv_sems, local_sems):
        self.ctx_size = ctx_size
        self.fsdp_size = fsdp_size
        self.ctx = lax.axis_index("ctx")
        self.fsdp = lax.axis_index("fsdp")
        self.send_sems = send_sems
        self.recv_sems = recv_sems
        self.local_sems = local_sems
        self.used = 0
        self.used_local = 0

    def slot(self):
        self.used += 1
        return self.used - 1

    def ctx_copy(self, slot, src, dst, peer):
        return pltpu.make_async_remote_copy(
            src_ref=src,
            dst_ref=dst,
            send_sem=self.send_sems.at[slot],
            recv_sem=self.recv_sems.at[slot],
            device_id={"ctx": peer},
            device_id_type=MESH,
        )

    def fsdp_copy(self, slot, src, dst, peer):
        return pltpu.make_async_remote_copy(
            src_ref=src,
            dst_ref=dst,
            send_sem=self.send_sems.at[slot],
            recv_sem=self.recv_sems.at[slot],
            device_id={"fsdp": peer},
            device_id_type=MESH,
        )

    def local(self, src, dst):
        self.used_local += 1
        return pltpu.make_async_copy(src, dst, self.local_sems.at[self.used_local - 1])

    def barrier(self, over_ctx, over_fsdp):
        sem = pltpu.get_barrier_semaphore()
        count = 0
        if over_ctx:
            for k in range(1, self.ctx_size):
                pl.semaphore_signal(sem, inc=1, device_id={"ctx": self.ctx ^ k}, device_id_type=MESH)
                count += 1
        if over_fsdp:
            for k in range(1, self.fsdp_size):
                pl.semaphore_signal(sem, inc=1, device_id={"fsdp": self.fsdp ^ k}, device_id_type=MESH)
                count += 1
        pl.semaphore_wait(sem, count)


def run_tasks(tasks):
    live = list(tasks)
    while live:
        left = []
        for task in live:
            try:
                next(task)
                left.append(task)
            except StopIteration:
                pass
        live = left


def gather_ctx(links, own, place):
    c, n = links.ctx, links.ctx_size
    line = n // 2
    pos = c // 2
    pair_slots = {}
    right_slots = [None] + [links.slot() for s in range(1, line)]
    left_slots = [None] + [links.slot() for s in range(1, line)]
    own_slot = links.slot()
    from_left_slots = [None] + [links.slot() for s in range(1, line)]
    from_right_slots = [None] + [links.slot() for s in range(1, line)]

    def block(step):
        return (c + 2 * step + n) % n

    def right(step):
        source = own if step == 1 else place(block(1 - step))
        return links.ctx_copy(right_slots[step], source, place(block(1 - step)), (c + 2) % n)

    def left(step):
        source = own if step == 1 else place(block(step - 1))
        return links.ctx_copy(left_slots[step], source, place(block(step - 1)), (c + n - 2) % n)

    def pair(step):
        if step == 0:
            return links.ctx_copy(own_slot, own, place(c), c ^ 1)
        slot = from_left_slots[-step] if step < 0 else from_right_slots[step]
        return links.ctx_copy(slot, place(block(step)), place(block(step)), c ^ 1)

    def arrived_from_left(step):
        return links.ctx_copy(right_slots[step], own, place(block(-step)), c ^ 1)

    def arrived_from_right(step):
        return links.ctx_copy(left_slots[step], own, place(block(step)), c ^ 1)

    if line > 1:
        @pl.when(pos < line - 1)
        def _():
            right(1).start()

        @pl.when(pos > 0)
        def _():
            left(1).start()

    pair(0).start()
    yield
    for step in range(1, line):
        @pl.when(pos >= step)
        def _():
            arrived_from_left(step).wait_recv()
            if step < line - 1:
                @pl.when(pos < line - 1)
                def _():
                    right(step + 1).start()
            pair(-step).start()

        @pl.when(pos + step < line)
        def _():
            arrived_from_right(step).wait_recv()
            if step < line - 1:
                @pl.when(pos > 0)
                def _():
                    left(step + 1).start()
            pair(step).start()

        yield
    pair(0).wait_send()
    links.ctx_copy(own_slot, own, place(c ^ 1), c ^ 1).wait_recv()
    for step in range(1, line):
        @pl.when(pos < line - 1)
        def _():
            @pl.when(pos >= step - 1)
            def _():
                right(step).wait_send()

        @pl.when(pos > 0)
        def _():
            @pl.when(pos + step - 1 < line)
            def _():
                left(step).wait_send()

        @pl.when(pos >= step)
        def _():
            pair(-step).wait_send()
            links.ctx_copy(from_left_slots[step], own, place(block(-step) ^ 1), c ^ 1).wait_recv()

        @pl.when(pos + step < line)
        def _():
            pair(step).wait_send()
            links.ctx_copy(from_right_slots[step], own, place(block(step) ^ 1), c ^ 1).wait_recv()


def spread_ctx(links, source, place, arrived):
    copies = []
    for k in reversed(range(1, links.ctx_size)):
        peer = links.ctx ^ k
        slot = links.slot()
        links.ctx_copy(slot, source(peer), place(), peer).start()
        copies.append((slot, peer))
    yield
    for slot, peer in copies:
        links.ctx_copy(slot, source(peer), arrived(peer), peer).wait()


def spread_fsdp(links, source, place, arrived):
    copies = []
    for k in reversed(range(1, links.fsdp_size)):
        peer = links.fsdp ^ k
        slot = links.slot()
        links.fsdp_copy(slot, source(peer), place(), peer).start()
        copies.append((slot, peer))
    yield
    for slot, peer in copies:
        links.fsdp_copy(slot, source(peer), arrived(peer), peer).wait()


def gather_fsdp(links, own, place):
    f = links.fsdp
    far = []
    for k in range(2, links.fsdp_size, 2):
        slot = links.slot()
        links.fsdp_copy(slot, own, place(f), f ^ k).start()
        far.append((k, slot))
    near = links.slot()
    links.fsdp_copy(near, own, place(f), f ^ 1).start()
    yield
    passed = []
    for k, slot in far:
        links.fsdp_copy(slot, own, place(f ^ k), f ^ k).wait_recv()
        onward = links.slot()
        links.fsdp_copy(onward, place(f ^ k), place(f ^ k), f ^ 1).start()
        passed.append((k, onward))
    yield
    links.fsdp_copy(near, own, place(f ^ 1), f ^ 1).wait()
    for k, slot in far:
        links.fsdp_copy(slot, own, place(f), f ^ k).wait_send()
    for k, onward in passed:
        links.fsdp_copy(onward, place(f ^ k), place(f ^ 1 ^ k), f ^ 1).wait()


def local_task(links, pairs):
    copies = [links.local(src, dst) for src, dst in pairs]
    for copy in copies:
        copy.start()
    yield
    yield
    yield
    for copy in copies:
        copy.wait()


def after(first, second):
    yield from first
    yield from second()


def exchange(name, number, sizes, make_tasks, operands, outs, over_ctx=True, over_fsdp=True, slots=96):
    ctx_size, fsdp_size = sizes

    def kernel(*refs):
        ins = refs[: len(operands)]
        results = refs[len(operands) : len(operands) + len(outs)]
        send_sems, recv_sems, local_sems = refs[len(operands) + len(outs) :]
        links = Links(ctx_size, fsdp_size, send_sems, recv_sems, local_sems)
        links.barrier(over_ctx, over_fsdp)
        run_tasks(make_tasks(links, ins, results))

    anywhere = pl.BlockSpec(memory_space=pl.ANY)
    return pl.pallas_call(
        kernel,
        in_specs=[anywhere] * len(operands),
        out_specs=[anywhere] * len(outs),
        out_shape=[jax.ShapeDtypeStruct(shape, dtype) for shape, dtype in outs],
        scratch_shapes=[
            pltpu.SemaphoreType.DMA((slots,)),
            pltpu.SemaphoreType.DMA((slots,)),
            pltpu.SemaphoreType.DMA((16,)),
        ],
        compiler_params=pltpu.CompilerParams(collective_id=number, has_side_effects=True),
        name=name,
    )(*operands)


def gather_all(sizes, tokens, seg, qkv_parts, out_rows, in_parts, mlp_parts, grad_out):
    n, fs = sizes
    bf16 = jnp.bfloat16

    def tasks(links, ins, outs):
        tokens_ref, seg_ref, qkv_ref, out_ref, in_ref, mlp_ref, grad_ref = ins
        tokens_all, seg_all, qkv_all, out_all, in_all, mlp_all, grad_all = outs
        c, f = links.ctx, links.fsdp
        chip, core = f // 2, f % 2
        staged = [
            (qkv_ref.at[c], qkv_all.at[c, f]),
            (out_ref, out_all.at[c, chip, core]),
            (in_ref.at[f], in_all.at[c, f]),
            (mlp_ref.at[f], mlp_all.at[c, f]),
        ]
        copies = [links.local(src, dst) for src, dst in staged]
        for copy in copies:
            copy.start()

        def weights(source_ref, all_ref, copy):
            def spread():
                yield from spread_fsdp(
                    links,
                    lambda peer: source_ref.at[peer],
                    lambda: all_ref.at[c, f],
                    lambda peer: all_ref.at[c, peer],
                )
                copy.wait()
                yield from gather_ctx(links, all_ref.at[c], lambda b: all_ref.at[b])
            return spread()

        def qkv():
            yield from spread_ctx(
                links,
                lambda peer: qkv_ref.at[peer],
                lambda: qkv_all.at[c, f],
                lambda peer: qkv_all.at[peer, f],
            )
            copies[0].wait()
            yield from gather_fsdp(links, qkv_all.at[:, f], lambda b: qkv_all.at[:, b])

        def out_weights():
            far = []
            for k in range(2, fs, 2):
                slot = links.slot()
                links.fsdp_copy(slot, out_ref, out_all.at[c, chip, core], f ^ k).start()
                far.append((slot, k))
            yield
            for slot, k in far:
                links.fsdp_copy(slot, out_ref, out_all.at[c, (f ^ k) // 2, core], f ^ k).wait()
            copies[1].wait()
            yield from gather_ctx(links, out_all.at[c, :, core], lambda b: out_all.at[b, :, core])
            slot = links.slot()
            links.fsdp_copy(slot, out_all.at[:, :, core], out_all.at[:, :, core], f ^ 1).start()
            yield
            links.fsdp_copy(slot, out_all.at[:, :, core], out_all.at[:, :, 1 - core], f ^ 1).wait()

        return [
            qkv(),
            gather_ctx(links, tokens_ref, lambda b: tokens_all.at[b]),
            spread_ctx(links, lambda peer: seg_ref, lambda: seg_all.at[c], lambda peer: seg_all.at[peer]),
            out_weights(),
            weights(in_ref, in_all, copies[2]),
            weights(mlp_ref, mlp_all, copies[3]),
            gather_fsdp(links, grad_ref, lambda b: grad_all.at[b]),
            local_task(
                links,
                [(tokens_ref, tokens_all.at[c]), (seg_ref, seg_all.at[c]), (grad_ref, grad_all.at[f])],
            ),
        ]

    outs = [
        ((n,) + tokens.shape, bf16),
        ((n,) + seg.shape, seg.dtype),
        ((n, fs) + qkv_parts.shape[1:], bf16),
        ((n, fs // 2, 2) + out_rows.shape, bf16),
        ((n, fs) + in_parts.shape[1:], bf16),
        ((n, fs) + mlp_parts.shape[1:], bf16),
        ((fs,) + grad_out.shape, bf16),
    ]
    return exchange(
        "gather_all",
        1,
        sizes,
        tasks,
        (tokens, seg, qkv_parts, out_rows, in_parts, mlp_parts, grad_out),
        outs,
        slots=12 * (n + fs),
    )


def swap_task(links, axis, src, out):
    me = links.ctx if axis == "ctx" else links.fsdp
    spread = spread_ctx if axis == "ctx" else spread_fsdp
    yield from spread(links, lambda peer: src.at[peer], lambda: out.at[me], lambda peer: out.at[peer])


def send_lines(links, src, out):
    c, n = links.ctx, links.ctx_size
    pos = c // 2
    slots = []
    for k in reversed(range(1, n // 2)):
        slot = links.slot()
        slots.append((slot, k))
        links.ctx_copy(slot, src.at[pos ^ k], out.at[pos], c ^ (2 * k)).start()
    yield
    for slot, k in slots:
        links.ctx_copy(slot, src.at[pos ^ k], out.at[pos ^ k], c ^ (2 * k)).wait()


def send_pairs(links, src, out):
    c, n = links.ctx, links.ctx_size
    slots = []
    for q in range(n // 2):
        slot = links.slot()
        slots.append(slot)
        links.ctx_copy(slot, src.at[q, 1 - c % 2], out.at[q], c ^ 1).start()
    yield
    for q, slot in enumerate(slots):
        links.ctx_copy(slot, src.at[q, 1 - c % 2], out.at[q], c ^ 1).wait()


def stage(name, number, sizes, kinds, arrays):
    def tasks(links, ins, outs):
        result = []
        own = []
        for kind, src, out in zip(kinds, ins, outs):
            if kind == "pair":
                result.append(send_pairs(links, src, out))
            elif kind == "line":
                pos = links.ctx // 2
                result.append(send_lines(links, src, out))
                own.append((src.at[pos], out.at[pos]))
            elif kind == "gather":
                result.append(gather_fsdp(links, src, lambda b, out=out: out.at[b]))
                own.append((src, out.at[links.fsdp]))
            else:
                me = links.ctx if kind == "ctx" else links.fsdp
                result.append(swap_task(links, kind, src, out))
                own.append((src.at[me], out.at[me]))
        return result + ([local_task(links, own)] if own else [])

    outs = []
    for kind, array in zip(kinds, arrays):
        shape = array.shape
        if kind == "pair":
            shape = shape[:1] + shape[2:]
        elif kind == "gather":
            shape = (sizes[1],) + shape
        outs.append((shape, array.dtype))
    return exchange(
        name,
        number,
        sizes,
        tasks,
        tuple(arrays),
        outs,
        over_ctx=any(kind in ("pair", "line", "ctx") for kind in kinds),
        over_fsdp=any(kind in ("fsdp", "gather") for kind in kinds),
        slots=len(arrays) * 2 * (sizes[0] + sizes[1]),
    )


def grad_blocks_kernel(side_ref, *refs):
    left_ref, in_ref, right_ref, mlp_ref = refs[:4]
    dims = (((0,), (0,)), ((), ()))
    left = left_ref[...].reshape(in_ref.shape[0], -1)
    right = right_ref[...].reshape(in_ref.shape[0], -1)
    grad_in = lax.dot_general(left, in_ref[...], dims, preferred_element_type=jnp.float32)
    grad_mlp = lax.dot_general(right, mlp_ref[...], dims, preferred_element_type=jnp.float32)
    if len(refs) == 8:
        grad_in = grad_in + refs[4][0].astype(jnp.float32)
        grad_mlp = grad_mlp + refs[5][0].astype(jnp.float32)
    refs[-2][0] = grad_in.astype(jnp.bfloat16)
    refs[-1][0] = grad_mlp.astype(jnp.bfloat16)


def grad_blocks(side, line, normed, grad_expanded, grad_out, product, received=()):
    tokens, width = normed.shape
    rows = width // (2 * line)
    picked = pl.BlockSpec((tokens, rows), lambda q, side_ref: (0, 2 * q + side_ref[0]))
    if rows % LANES:
        picked = pl.BlockSpec((1, tokens, rows), lambda q, side_ref: (2 * q + side_ref[0], 0, 0))
        normed = jnp.transpose(normed.reshape(tokens, 2 * line, rows), (1, 0, 2))
        grad_out = jnp.transpose(grad_out.reshape(tokens, 2 * line, rows), (1, 0, 2))
    wide = [grad_expanded.shape[1], product.shape[1]]
    whole = [pl.BlockSpec((tokens, w), lambda q, side_ref: (0, 0)) for w in wide]
    block = [pl.BlockSpec((1, rows, w), lambda q, side_ref: (q, 0, 0)) for w in wide]
    return pl.pallas_call(
        grad_blocks_kernel,
        grid_spec=pltpu.PrefetchScalarGridSpec(
            num_scalar_prefetch=1,
            grid=(line,),
            in_specs=[picked, whole[0], picked, whole[1]] + block[: len(received)],
            out_specs=block,
        ),
        out_shape=[jax.ShapeDtypeStruct((line, rows, w), jnp.bfloat16) for w in wide],
        cost_estimate=pl.CostEstimate(
            flops=tokens * width * sum(wide), bytes_accessed=6 * tokens * width, transcendentals=0
        ),
        name="grad_blocks",
    )(side, normed, grad_expanded, grad_out, product, *received)


def pick(array, index, axis):
    return lax.dynamic_index_in_dim(array, index, axis, keepdims=False)


def body(
    ctx_size,
    fsdp_size,
    inputs,
    segment_ids,
    gain_attn,
    w_qkv,
    w_out_attn,
    gain_mlp,
    w_in,
    w_out_mlp,
    cotangent,
):
    tok_count, width = inputs.shape[1:]
    heads = HEADS
    head_size = HD
    scale = 1.0 / math.sqrt(head_size)
    hidden_units = w_out_mlp.shape[0]
    row_count = ctx_size * tok_count
    own_heads = heads // ctx_size
    own_width = own_heads * head_size
    weight_rows = w_qkv.shape[0]
    own_hidden = hidden_units // fsdp_size
    own_out = width // fsdp_size
    line = ctx_size // 2
    block_rows = width // ctx_size
    sizes = (ctx_size, fsdp_size)
    bf16 = jnp.bfloat16
    f32 = jnp.float32
    ctx_index = lax.axis_index("ctx")
    parity = ctx_index % 2
    pos = ctx_index // 2

    qkv_parts = jnp.transpose(
        w_qkv.reshape(weight_rows, 3, ctx_size, own_width), (2, 0, 1, 3)
    ).reshape(ctx_size, weight_rows, 3 * own_width)
    gains_own = jnp.pad(jnp.stack([gain_attn, gain_mlp], axis=1), ((0, 0), (0, LANES - 2)))
    qkv_parts = jnp.concatenate(
        [qkv_parts, jnp.broadcast_to(gains_own, (ctx_size, weight_rows, LANES))], axis=2
    )
    in_parts = jnp.transpose(
        w_in.reshape(weight_rows, 2, fsdp_size, own_hidden), (2, 0, 1, 3)
    ).reshape(fsdp_size, weight_rows, 2 * own_hidden)
    mlp_parts = jnp.transpose(w_out_mlp.reshape(fsdp_size, own_hidden, weight_rows), (0, 2, 1))
    seg_own = jnp.broadcast_to(segment_ids.astype(f32), (8, tok_count))

    tokens_all, seg_all, qkv_all, out_all, in_all, mlp_all, grad_out_group = gather_all(
        sizes, inputs[0], seg_own, qkv_parts, w_out_attn, in_parts, mlp_parts, cotangent[0]
    )
    qkv_got = qkv_all.reshape(width, 3 * own_width + LANES)
    qkv_mine = qkv_got[:, : 3 * own_width]
    gains = qkv_got[:, 3 * own_width : 3 * own_width + 2].astype(f32).T
    gain_first = gains[0]
    gain_second = gains[1]
    attn_full = out_all.reshape(width, width)
    in_mine = in_all.reshape(width, 2 * own_hidden)
    mlp_turned = mlp_all.reshape(width, own_hidden)

    seg_row = seg_all[:, 0].reshape(1, row_count)
    seg_col = seg_row.reshape(row_count, 1)
    row_tokens = tokens_all.reshape(row_count, width).astype(f32)
    row_normed, unused = layer_norm(row_tokens)
    row_normed_attn = (row_normed * gain_first).astype(bf16)
    tokens = inputs[0].astype(f32)
    normed_one, scale_one = layer_norm(tokens)

    projected_cols = jnp.einsum(
        "de,td->et", qkv_mine, row_normed_attn, preferred_element_type=f32
    ).reshape(3, own_heads, head_size, row_count)
    positions = jnp.arange(row_count, dtype=jnp.int32).astype(f32)
    cosine, sine = rope_columns(positions, head_size)
    query_cols = rotate_cols(projected_cols[0], cosine, sine).astype(bf16)
    key_cols = rotate_cols(projected_cols[1], cosine, sine).astype(bf16)
    value_cols = projected_cols[2].astype(bf16)
    row_attended, log_total = attend(query_cols, key_cols, value_cols, seg_col, seg_row, scale)

    (attended,) = stage(
        "swap_attended",
        2,
        sizes,
        ("ctx",),
        (row_attended.reshape(own_width, row_count).T.reshape(ctx_size, tok_count, own_width),),
    )
    attended = jnp.transpose(attended, (1, 0, 2)).reshape(tok_count, width)
    residual = tokens + jnp.dot(attended, attn_full, preferred_element_type=f32)
    normed_two, scale_two = layer_norm(residual)
    normed_mlp = (normed_two * gain_second).astype(bf16)
    (normed_group,) = stage("gather_normed", 3, sizes, ("gather",), (normed_mlp,))
    group = fsdp_size * tok_count
    normed_group = normed_group.reshape(group, width)
    grad_out_group = grad_out_group.reshape(group, width)

    expanded = jnp.dot(normed_group, in_mine, preferred_element_type=f32)
    pre_act = expanded[:, :own_hidden]
    gate_part = expanded[:, own_hidden:]
    activated = jax.nn.gelu(pre_act, approximate=False)
    product = (activated * gate_part).astype(bf16)
    grad_product = jnp.einsum("td,df->tf", grad_out_group, mlp_turned, preferred_element_type=f32)
    grad_expanded = jnp.concatenate(
        [grad_product * gate_part * gelu_slope(pre_act), grad_product * activated], axis=1
    ).astype(bf16)
    grad_normed_part = jnp.einsum(
        "tf,df->td", grad_expanded, in_mine, preferred_element_type=f32
    ).astype(bf16)
    out_part = jnp.einsum("tf,df->td", product, mlp_turned, preferred_element_type=f32).astype(bf16)

    (grad_normed_parts,) = stage(
        "swap_grad_normed",
        4,
        sizes,
        ("fsdp",),
        (grad_normed_part.reshape(fsdp_size, tok_count, width),),
    )
    grad_normed_mlp = jnp.sum(grad_normed_parts.astype(f32), axis=0)

    side = jnp.reshape(parity, (1,)).astype(jnp.int32)
    swap_pair = [(i, i ^ 1) for i in range(ctx_size)]
    sent = grad_blocks(1 - side, line, normed_group, grad_expanded, grad_out_group, product)
    received = [lax.ppermute(blocks, "ctx", swap_pair) for blocks in sent]

    grad_gain_two = jnp.sum(grad_normed_mlp * normed_two, axis=0)
    grad_residual = cotangent[0].astype(f32) + norm_back(
        grad_normed_mlp * gain_second, normed_two, scale_two
    )
    residual_half = grad_residual.astype(bf16)
    grad_attended = jnp.einsum(
        "te,de->td", residual_half, attn_full, preferred_element_type=f32
    ).astype(bf16)
    row_grad, residual_cols, attended_group = stage(
        "swap_grad_attended",
        5,
        sizes,
        ("ctx", "fsdp", "gather"),
        (
            jnp.transpose(grad_attended.reshape(tok_count, ctx_size, own_width), (1, 0, 2)),
            jnp.transpose(residual_half.reshape(tok_count, fsdp_size, own_out), (1, 0, 2)),
            attended,
        ),
    )
    grad_attn_part = jnp.einsum(
        "td,te->de",
        attended_group.reshape(group, width),
        residual_cols.reshape(group, own_out),
        preferred_element_type=f32,
    ).reshape(line, 2, block_rows, own_out)
    row_grad_cols = row_grad.reshape(row_count, own_width).T.reshape(
        own_heads, head_size, row_count
    )
    grad_query, grad_key, grad_value = attend_grads(
        query_cols,
        key_cols,
        value_cols,
        seg_col,
        seg_row,
        log_total,
        row_grad_cols,
        row_attended,
        scale,
    )
    grad_proj_cols = (
        jnp.stack(
            [
                unrotate_cols(grad_query, cosine, sine),
                unrotate_cols(grad_key, cosine, sine),
                grad_value,
            ],
            axis=0,
        )
        .astype(bf16)
        .reshape(3 * own_width, row_count)
    )
    row_grad_normed = jnp.einsum("de,et->td", qkv_mine, grad_proj_cols, preferred_element_type=f32)
    grad_gain_part = jnp.sum(row_grad_normed * row_normed, axis=0)
    gain_columns = jnp.pad(
        jnp.stack([grad_gain_part, grad_gain_two], axis=1), ((0, 0), (0, LANES - 2))
    )
    qkv_terms = jnp.concatenate(
        [
            jnp.einsum("td,et->de", row_normed_attn, grad_proj_cols, preferred_element_type=f32),
            gain_columns,
        ],
        axis=1,
    ).astype(bf16)
    qkv_width = 3 * own_width + LANES
    qkv_terms = jnp.transpose(
        qkv_terms.reshape(ctx_size, fsdp_size, weight_rows, qkv_width), (1, 0, 2, 3)
    )
    row_grad_blocks = row_grad_normed.reshape(line, 2, tok_count, width)
    row_grad_half = row_grad_blocks.astype(bf16)
    grad_attn_half = grad_attn_part.astype(bf16)
    in_sum, mlp_sum = grad_blocks(
        side, line, normed_group, grad_expanded, grad_out_group, product, received
    )
    row_other, attn_other, in_lines, mlp_lines, qkv_got_terms, out_parts = stage(
        "pair_stage",
        6,
        sizes,
        ("pair", "pair", "line", "line", "fsdp", "fsdp"),
        (
            row_grad_half,
            grad_attn_half,
            in_sum,
            mlp_sum,
            qkv_terms,
            out_part.reshape(fsdp_size, tok_count, width),
        ),
    )
    block_out = (residual + jnp.sum(out_parts.astype(f32), axis=0)).astype(bf16)
    row_sum = (pick(row_grad_half, parity, 1).astype(f32) + row_other.astype(f32)).astype(bf16)
    attn_sum = (pick(grad_attn_half, parity, 1).astype(f32) + attn_other.astype(f32)).astype(bf16)
    qkv_half = jnp.sum(qkv_got_terms.astype(f32), axis=0).astype(bf16)
    grad_in_block = jnp.sum(in_lines.astype(f32), axis=0).astype(bf16)
    grad_mlp_block = jnp.sum(mlp_lines.astype(f32), axis=0).astype(bf16)
    row_lines, attn_lines, qkv_lines, in_got, mlp_got = stage(
        "line_stage",
        7,
        sizes,
        ("line", "line", "ctx", "fsdp", "fsdp"),
        (
            row_sum,
            attn_sum,
            qkv_half,
            grad_in_block.reshape(fsdp_size, weight_rows, 2 * own_hidden),
            grad_mlp_block.reshape(fsdp_size, weight_rows, own_hidden),
        ),
    )
    grad_normed_attn = jnp.sum(row_lines.astype(f32), axis=0)
    grad_attn_block = jnp.sum(attn_lines.astype(f32), axis=0).astype(bf16)
    grad_tokens = (
        grad_residual + norm_back(grad_normed_attn * gain_first, normed_one, scale_one)
    ).astype(bf16)
    grad_qkv_rows = jnp.transpose(
        qkv_lines[:, :, : 3 * own_width].astype(f32).reshape(ctx_size, weight_rows, 3, own_width),
        (1, 2, 0, 3),
    ).reshape(weight_rows, 3 * width)
    gain_sums = jnp.sum(qkv_lines[:, :, 3 * own_width : 3 * own_width + 2].astype(f32), axis=0)

    (attn_got,) = stage(
        "swap_weight_grads",
        8,
        sizes,
        ("fsdp",),
        (grad_attn_block.reshape(fsdp_size, weight_rows, own_out),),
    )
    grad_in_rows = jnp.transpose(
        in_got.astype(f32).reshape(fsdp_size, weight_rows, 2, own_hidden), (1, 2, 0, 3)
    ).reshape(weight_rows, 2 * hidden_units)
    grad_mlp_cols = jnp.transpose(mlp_got.astype(f32), (0, 2, 1)).reshape(hidden_units, weight_rows)
    grad_attn_rows = jnp.transpose(attn_got.astype(f32), (1, 0, 2)).reshape(weight_rows, width)
    return (
        block_out[None],
        grad_tokens[None],
        grad_qkv_rows,
        grad_attn_rows,
        grad_in_rows,
        grad_mlp_cols,
        gain_sums[:, 0],
        gain_sums[:, 1],
    )


def solution(mesh):
    in_specs = (
        P("fsdp", "ctx", None),
        P("fsdp", "ctx"),
        P(("ctx", "fsdp")),
        P(("ctx", "fsdp"), None),
        P(("ctx", "fsdp"), None),
        P(("ctx", "fsdp")),
        P(("ctx", "fsdp"), None),
        P(None, ("ctx", "fsdp")),
        P("fsdp", "ctx", None),
    )
    out_specs = (
        P("fsdp", "ctx", None),
        P("fsdp", "ctx", None),
        P(("ctx", "fsdp"), None),
        P(("ctx", "fsdp"), None),
        P(("ctx", "fsdp"), None),
        P(None, ("ctx", "fsdp")),
        P(("ctx", "fsdp")),
        P(("ctx", "fsdp")),
    )
    step = functools.partial(body, mesh.shape["ctx"], mesh.shape["fsdp"])
    return jax.shard_map(step, mesh=mesh, in_specs=in_specs, out_specs=out_specs, check_vma=False)
```

```python
import functools
import math

import jax
import jax.numpy as jnp
from jax import lax
from jax.experimental import pallas as pl
from jax.experimental.pallas import tpu as pltpu
from jax.sharding import PartitionSpec as P

HEADS = 16
HD = 64


EPSILON = 1e-05
ROPE_BASE = 160000.0
MASKED = -1e30


def layer_norm(values):
    center = values - jnp.mean(values, axis=-1, keepdims=True)
    scaled = lax.rsqrt(jnp.mean(center * center, axis=-1, keepdims=True) + EPSILON)
    return (center * scaled, scaled)


def norm_back(grad_norm, normed, scaled):
    return scaled * (
        grad_norm
        - jnp.mean(grad_norm, axis=-1, keepdims=True)
        - normed * jnp.mean(grad_norm * normed, axis=-1, keepdims=True)
    )


def rope_columns(positions, head_size):
    freqs = ROPE_BASE ** (-jnp.arange(0, head_size, 2, dtype=jnp.float32) / head_size)
    angles = freqs[:, None] * positions[None, :]
    cosine = jnp.concatenate([jnp.cos(angles), jnp.cos(angles)], axis=0)
    sine = jnp.concatenate([jnp.sin(angles), jnp.sin(angles)], axis=0)
    return (cosine[None], sine[None])


def rotate_cols(values, cosine, sine):
    half = values.shape[1] // 2
    turned = jnp.concatenate([-values[:, half:], values[:, :half]], axis=1)
    return values * cosine + turned * sine


def unrotate_cols(grads, cosine, sine):
    half = grads.shape[1] // 2
    weighted = grads * sine
    turned = jnp.concatenate([weighted[:, half:], -weighted[:, :half]], axis=1)
    return grads * cosine + turned


def gelu_slope(values):
    return (
        0.5 * (1.0 + lax.erf(values * 0.7071067811865476))
        + values * jnp.exp(-0.5 * values * values) * 0.3989422804014327
    )


LANES = 128
QUERY_BLOCK = 256


def masked_scores(query, key, same, scale):
    scores = lax.dot_general(query, key, (((0,), (0,)), ((), ())), preferred_element_type=jnp.float32)
    return jnp.where(same, scores * scale, MASKED)


def attend_kernel(scale, query_ref, key_ref, value_ref, seg_own_ref, seg_ref, out_ref, log_ref):
    same = seg_own_ref[...] == seg_ref[...]
    scores = masked_scores(query_ref[0], key_ref[0], same, scale)
    peak = jnp.max(scores, axis=-1, keepdims=True)
    log_total = peak + jnp.log(jnp.sum(jnp.exp(scores - peak), axis=-1, keepdims=True))
    log_ref[0] = log_total
    probs = jnp.exp(scores - log_total).astype(jnp.bfloat16)
    out_ref[0] = lax.dot_general(
        value_ref[0], probs, (((1,), (1,)), ((), ())), preferred_element_type=jnp.float32
    ).astype(jnp.bfloat16)


def attend_grad_kernel(
    scale,
    query_ref,
    key_ref,
    value_ref,
    seg_own_ref,
    seg_ref,
    log_ref,
    grad_ref,
    attended_ref,
    query_grad_ref,
    key_grad_ref,
    value_grad_ref,
):
    @pl.when(pl.program_id(1) == 0)
    def _():
        key_grad_ref[...] = jnp.zeros_like(key_grad_ref)
        value_grad_ref[...] = jnp.zeros_like(value_grad_ref)

    query = query_ref[0]
    grad = grad_ref[0]
    key = key_ref[0]
    dots_row = jnp.sum(
        grad.astype(jnp.float32) * attended_ref[0].astype(jnp.float32), axis=0, keepdims=True
    )
    dots = jnp.transpose(jnp.broadcast_to(dots_row, (8, dots_row.shape[1])))[:, :1]
    same = seg_own_ref[...] == seg_ref[...]
    probs = jnp.exp(masked_scores(query, key, same, scale) - log_ref[0])
    grad_probs = lax.dot_general(
        grad, value_ref[0], (((0,), (0,)), ((), ())), preferred_element_type=jnp.float32
    )
    grad_scores = (probs * (grad_probs - dots)).astype(jnp.bfloat16)
    query_grad_ref[0] = scale * lax.dot_general(
        key, grad_scores, (((1,), (1,)), ((), ())), preferred_element_type=jnp.float32
    )
    key_grad_ref[0] += scale * lax.dot_general(
        query, grad_scores, (((1,), (0,)), ((), ())), preferred_element_type=jnp.float32
    )
    value_grad_ref[0] += lax.dot_general(
        grad, probs.astype(jnp.bfloat16), (((1,), (0,)), ((), ())), preferred_element_type=jnp.float32
    )


def attention_specs(head_size, row_count, block):
    part = pl.BlockSpec((1, head_size, block), lambda h, b: (h, 0, b))
    full = pl.BlockSpec((1, head_size, row_count), lambda h, b: (h, 0, 0))
    seg_own = pl.BlockSpec((block, 1), lambda h, b: (b, 0))
    seg_all = pl.BlockSpec((1, row_count), lambda h, b: (0, 0))
    log = pl.BlockSpec((1, block, 1), lambda h, b: (h, b, 0))
    return part, full, seg_own, seg_all, log


def attend(query_cols, key_cols, value_cols, seg_col, seg_row, scale):
    heads, head_size, row_count = query_cols.shape
    block = min(QUERY_BLOCK, row_count)
    part, full, own, every, log = attention_specs(head_size, row_count, block)
    return pl.pallas_call(
        lambda *refs: attend_kernel(scale, *refs),
        grid=(heads, row_count // block),
        in_specs=[part, full, full, own, every],
        out_specs=[part, log],
        out_shape=[
            jax.ShapeDtypeStruct((heads, head_size, row_count), jnp.bfloat16),
            jax.ShapeDtypeStruct((heads, row_count, 1), jnp.float32),
        ],
        name="attend",
    )(query_cols, key_cols, value_cols, seg_col, seg_row)


def attend_grads(
    query_cols, key_cols, value_cols, seg_col, seg_row, log_total, grad_cols, attended_cols, scale
):
    heads, head_size, row_count = query_cols.shape
    block = min(QUERY_BLOCK, row_count)
    part, full, own, every, log = attention_specs(head_size, row_count, block)
    grads = jax.ShapeDtypeStruct((heads, head_size, row_count), jnp.float32)
    return pl.pallas_call(
        lambda *refs: attend_grad_kernel(scale, *refs),
        grid=(heads, row_count // block),
        in_specs=[part, full, full, own, every, log, part, part],
        out_specs=[part, full, full],
        out_shape=[grads, grads, grads],
        name="attend_grads",
    )(query_cols, key_cols, value_cols, seg_col, seg_row, log_total, grad_cols, attended_cols)


MESH = pl.DeviceIdType.MESH


class Links:
    def __init__(self, ctx_size, fsdp_size, send_sems, recv_sems, local_sems):
        self.ctx_size = ctx_size
        self.fsdp_size = fsdp_size
        self.ctx = lax.axis_index("ctx")
        self.fsdp = lax.axis_index("fsdp")
        self.send_sems = send_sems
        self.recv_sems = recv_sems
        self.local_sems = local_sems
        self.used = 0
        self.used_local = 0

    def slot(self):
        self.used += 1
        return self.used - 1

    def ctx_copy(self, slot, src, dst, peer):
        return pltpu.make_async_remote_copy(
            src_ref=src,
            dst_ref=dst,
            send_sem=self.send_sems.at[slot],
            recv_sem=self.recv_sems.at[slot],
            device_id={"ctx": peer},
            device_id_type=MESH,
        )

    def fsdp_copy(self, slot, src, dst, peer):
        return pltpu.make_async_remote_copy(
            src_ref=src,
            dst_ref=dst,
            send_sem=self.send_sems.at[slot],
            recv_sem=self.recv_sems.at[slot],
            device_id={"fsdp": peer},
            device_id_type=MESH,
        )

    def local(self, src, dst):
        self.used_local += 1
        return pltpu.make_async_copy(src, dst, self.local_sems.at[self.used_local - 1])

    def barrier(self, over_ctx, over_fsdp):
        sem = pltpu.get_barrier_semaphore()
        count = 0
        if over_ctx:
            for k in range(1, self.ctx_size):
                pl.semaphore_signal(sem, inc=1, device_id={"ctx": self.ctx ^ k}, device_id_type=MESH)
                count += 1
        if over_fsdp:
            for k in range(1, self.fsdp_size):
                pl.semaphore_signal(sem, inc=1, device_id={"fsdp": self.fsdp ^ k}, device_id_type=MESH)
                count += 1
        pl.semaphore_wait(sem, count)


def run_tasks(tasks):
    live = list(tasks)
    while live:
        left = []
        for task in live:
            try:
                next(task)
                left.append(task)
            except StopIteration:
                pass
        live = left


def gather_ctx(links, own, place):
    c, n = links.ctx, links.ctx_size
    line = n // 2
    pos = c // 2
    pair_slots = {}
    right_slots = [None] + [links.slot() for s in range(1, line)]
    left_slots = [None] + [links.slot() for s in range(1, line)]
    own_slot = links.slot()
    from_left_slots = [None] + [links.slot() for s in range(1, line)]
    from_right_slots = [None] + [links.slot() for s in range(1, line)]

    def block(step):
        return (c + 2 * step + n) % n

    def right(step):
        source = own if step == 1 else place(block(1 - step))
        return links.ctx_copy(right_slots[step], source, place(block(1 - step)), (c + 2) % n)

    def left(step):
        source = own if step == 1 else place(block(step - 1))
        return links.ctx_copy(left_slots[step], source, place(block(step - 1)), (c + n - 2) % n)

    def pair(step):
        if step == 0:
            return links.ctx_copy(own_slot, own, place(c), c ^ 1)
        slot = from_left_slots[-step] if step < 0 else from_right_slots[step]
        return links.ctx_copy(slot, place(block(step)), place(block(step)), c ^ 1)

    def arrived_from_left(step):
        return links.ctx_copy(right_slots[step], own, place(block(-step)), c ^ 1)

    def arrived_from_right(step):
        return links.ctx_copy(left_slots[step], own, place(block(step)), c ^ 1)

    if line > 1:
        @pl.when(pos < line - 1)
        def _():
            right(1).start()

        @pl.when(pos > 0)
        def _():
            left(1).start()

    pair(0).start()
    yield
    for step in range(1, line):
        @pl.when(pos >= step)
        def _():
            arrived_from_left(step).wait_recv()
            if step < line - 1:
                @pl.when(pos < line - 1)
                def _():
                    right(step + 1).start()
            pair(-step).start()

        @pl.when(pos + step < line)
        def _():
            arrived_from_right(step).wait_recv()
            if step < line - 1:
                @pl.when(pos > 0)
                def _():
                    left(step + 1).start()
            pair(step).start()

        yield
    pair(0).wait_send()
    links.ctx_copy(own_slot, own, place(c ^ 1), c ^ 1).wait_recv()
    for step in range(1, line):
        @pl.when(pos < line - 1)
        def _():
            @pl.when(pos >= step - 1)
            def _():
                right(step).wait_send()

        @pl.when(pos > 0)
        def _():
            @pl.when(pos + step - 1 < line)
            def _():
                left(step).wait_send()

        @pl.when(pos >= step)
        def _():
            pair(-step).wait_send()
            links.ctx_copy(from_left_slots[step], own, place(block(-step) ^ 1), c ^ 1).wait_recv()

        @pl.when(pos + step < line)
        def _():
            pair(step).wait_send()
            links.ctx_copy(from_right_slots[step], own, place(block(step) ^ 1), c ^ 1).wait_recv()


def spread_ctx(links, source, place, arrived):
    copies = []
    for k in reversed(range(1, links.ctx_size)):
        peer = links.ctx ^ k
        slot = links.slot()
        links.ctx_copy(slot, source(peer), place(), peer).start()
        copies.append((slot, peer))
    yield
    for slot, peer in copies:
        links.ctx_copy(slot, source(peer), arrived(peer), peer).wait()


def spread_fsdp(links, source, place, arrived):
    copies = []
    for k in reversed(range(1, links.fsdp_size)):
        peer = links.fsdp ^ k
        slot = links.slot()
        links.fsdp_copy(slot, source(peer), place(), peer).start()
        copies.append((slot, peer))
    yield
    for slot, peer in copies:
        links.fsdp_copy(slot, source(peer), arrived(peer), peer).wait()


def gather_fsdp(links, own, place):
    f = links.fsdp
    far = []
    for k in range(2, links.fsdp_size, 2):
        slot = links.slot()
        links.fsdp_copy(slot, own, place(f), f ^ k).start()
        far.append((k, slot))
    near = links.slot()
    links.fsdp_copy(near, own, place(f), f ^ 1).start()
    yield
    passed = []
    for k, slot in far:
        links.fsdp_copy(slot, own, place(f ^ k), f ^ k).wait_recv()
        onward = links.slot()
        links.fsdp_copy(onward, place(f ^ k), place(f ^ k), f ^ 1).start()
        passed.append((k, onward))
    yield
    links.fsdp_copy(near, own, place(f ^ 1), f ^ 1).wait()
    for k, slot in far:
        links.fsdp_copy(slot, own, place(f), f ^ k).wait_send()
    for k, onward in passed:
        links.fsdp_copy(onward, place(f ^ k), place(f ^ 1 ^ k), f ^ 1).wait()


def local_task(links, pairs):
    copies = [links.local(src, dst) for src, dst in pairs]
    for copy in copies:
        copy.start()
    yield
    yield
    yield
    for copy in copies:
        copy.wait()


def after(first, second):
    yield from first
    yield from second()


def exchange(name, number, sizes, make_tasks, operands, outs, over_ctx=True, over_fsdp=True, slots=96):
    ctx_size, fsdp_size = sizes

    def kernel(*refs):
        ins = refs[: len(operands)]
        results = refs[len(operands) : len(operands) + len(outs)]
        send_sems, recv_sems, local_sems = refs[len(operands) + len(outs) :]
        links = Links(ctx_size, fsdp_size, send_sems, recv_sems, local_sems)
        links.barrier(over_ctx, over_fsdp)
        run_tasks(make_tasks(links, ins, results))

    anywhere = pl.BlockSpec(memory_space=pl.ANY)
    return pl.pallas_call(
        kernel,
        in_specs=[anywhere] * len(operands),
        out_specs=[anywhere] * len(outs),
        out_shape=[jax.ShapeDtypeStruct(shape, dtype) for shape, dtype in outs],
        scratch_shapes=[
            pltpu.SemaphoreType.DMA((slots,)),
            pltpu.SemaphoreType.DMA((slots,)),
            pltpu.SemaphoreType.DMA((16,)),
        ],
        compiler_params=pltpu.CompilerParams(collective_id=number, has_side_effects=True),
        name=name,
    )(*operands)


def gather_all(sizes, tokens, seg, qkv_parts, out_rows, in_parts, mlp_parts, grad_out):
    n, fs = sizes
    bf16 = jnp.bfloat16

    def tasks(links, ins, outs):
        tokens_ref, seg_ref, qkv_ref, out_ref, in_ref, mlp_ref, grad_ref = ins
        tokens_all, seg_all, qkv_all, out_all, in_all, mlp_all, grad_all = outs
        c, f = links.ctx, links.fsdp
        chip, core = f // 2, f % 2
        staged = [
            (qkv_ref.at[c], qkv_all.at[c, f]),
            (out_ref, out_all.at[c, chip, core]),
            (in_ref.at[f], in_all.at[c, f]),
            (mlp_ref.at[f], mlp_all.at[c, f]),
        ]
        copies = [links.local(src, dst) for src, dst in staged]
        for copy in copies:
            copy.start()

        def weights(source_ref, all_ref, copy):
            def spread():
                yield from spread_fsdp(
                    links,
                    lambda peer: source_ref.at[peer],
                    lambda: all_ref.at[c, f],
                    lambda peer: all_ref.at[c, peer],
                )
                copy.wait()
                yield from gather_ctx(links, all_ref.at[c], lambda b: all_ref.at[b])
            return spread()

        def qkv():
            yield from spread_ctx(
                links,
                lambda peer: qkv_ref.at[peer],
                lambda: qkv_all.at[c, f],
                lambda peer: qkv_all.at[peer, f],
            )
            copies[0].wait()
            yield from gather_fsdp(links, qkv_all.at[:, f], lambda b: qkv_all.at[:, b])

        def out_weights():
            copies[1].wait()
            yield from gather_ctx(links, out_ref, lambda b: out_all.at[b, chip, core])
            mine = out_all.at[:, chip, core]
            far = []
            for k in range(2, fs, 2):
                slot = links.slot()
                links.fsdp_copy(slot, mine, mine, f ^ k).start()
                far.append((slot, k))
            yield
            for slot, k in far:
                links.fsdp_copy(slot, mine, out_all.at[:, (f ^ k) // 2, core], f ^ k).wait()
            slot = links.slot()
            links.fsdp_copy(slot, out_all.at[:, :, core], out_all.at[:, :, core], f ^ 1).start()
            yield
            links.fsdp_copy(slot, out_all.at[:, :, core], out_all.at[:, :, 1 - core], f ^ 1).wait()

        return [
            qkv(),
            gather_ctx(links, tokens_ref, lambda b: tokens_all.at[b]),
            spread_ctx(links, lambda peer: seg_ref, lambda: seg_all.at[c], lambda peer: seg_all.at[peer]),
            out_weights(),
            weights(in_ref, in_all, copies[2]),
            weights(mlp_ref, mlp_all, copies[3]),
            gather_fsdp(links, grad_ref, lambda b: grad_all.at[b]),
            local_task(
                links,
                [(tokens_ref, tokens_all.at[c]), (seg_ref, seg_all.at[c]), (grad_ref, grad_all.at[f])],
            ),
        ]

    outs = [
        ((n,) + tokens.shape, bf16),
        ((n,) + seg.shape, seg.dtype),
        ((n, fs) + qkv_parts.shape[1:], bf16),
        ((n, fs // 2, 2) + out_rows.shape, bf16),
        ((n, fs) + in_parts.shape[1:], bf16),
        ((n, fs) + mlp_parts.shape[1:], bf16),
        ((fs,) + grad_out.shape, bf16),
    ]
    return exchange(
        "gather_all",
        1,
        sizes,
        tasks,
        (tokens, seg, qkv_parts, out_rows, in_parts, mlp_parts, grad_out),
        outs,
        slots=12 * (n + fs),
    )


def swap_task(links, axis, src, out):
    me = links.ctx if axis == "ctx" else links.fsdp
    spread = spread_ctx if axis == "ctx" else spread_fsdp
    yield from spread(links, lambda peer: src.at[peer], lambda: out.at[me], lambda peer: out.at[peer])


def send_lines(links, src, out):
    c, n = links.ctx, links.ctx_size
    pos = c // 2
    slots = []
    for k in reversed(range(1, n // 2)):
        slot = links.slot()
        slots.append((slot, k))
        links.ctx_copy(slot, src.at[pos ^ k], out.at[pos], c ^ (2 * k)).start()
    yield
    for slot, k in slots:
        links.ctx_copy(slot, src.at[pos ^ k], out.at[pos ^ k], c ^ (2 * k)).wait()


def send_pairs(links, src, out):
    c, n = links.ctx, links.ctx_size
    slots = []
    for q in range(n // 2):
        slot = links.slot()
        slots.append(slot)
        links.ctx_copy(slot, src.at[q, 1 - c % 2], out.at[q], c ^ 1).start()
    yield
    for q, slot in enumerate(slots):
        links.ctx_copy(slot, src.at[q, 1 - c % 2], out.at[q], c ^ 1).wait()


def stage(name, number, sizes, kinds, arrays):
    def tasks(links, ins, outs):
        result = []
        own = []
        for kind, src, out in zip(kinds, ins, outs):
            if kind == "pair":
                result.append(send_pairs(links, src, out))
            elif kind == "line":
                pos = links.ctx // 2
                result.append(send_lines(links, src, out))
                own.append((src.at[pos], out.at[pos]))
            elif kind == "gather":
                result.append(gather_fsdp(links, src, lambda b, out=out: out.at[b]))
                own.append((src, out.at[links.fsdp]))
            else:
                me = links.ctx if kind == "ctx" else links.fsdp
                result.append(swap_task(links, kind, src, out))
                own.append((src.at[me], out.at[me]))
        return result + ([local_task(links, own)] if own else [])

    outs = []
    for kind, array in zip(kinds, arrays):
        shape = array.shape
        if kind == "pair":
            shape = shape[:1] + shape[2:]
        elif kind == "gather":
            shape = (sizes[1],) + shape
        outs.append((shape, array.dtype))
    return exchange(
        name,
        number,
        sizes,
        tasks,
        tuple(arrays),
        outs,
        over_ctx=any(kind in ("pair", "line", "ctx") for kind in kinds),
        over_fsdp=any(kind in ("fsdp", "gather") for kind in kinds),
        slots=len(arrays) * 2 * (sizes[0] + sizes[1]),
    )


def grad_blocks_kernel(side_ref, *refs):
    left_ref, in_ref, right_ref, mlp_ref = refs[:4]
    dims = (((0,), (0,)), ((), ()))
    left = left_ref[...].reshape(in_ref.shape[0], -1)
    right = right_ref[...].reshape(in_ref.shape[0], -1)
    grad_in = lax.dot_general(left, in_ref[...], dims, preferred_element_type=jnp.float32)
    grad_mlp = lax.dot_general(right, mlp_ref[...], dims, preferred_element_type=jnp.float32)
    if len(refs) == 8:
        grad_in = grad_in + refs[4][0].astype(jnp.float32)
        grad_mlp = grad_mlp + refs[5][0].astype(jnp.float32)
    refs[-2][0] = grad_in.astype(jnp.bfloat16)
    refs[-1][0] = grad_mlp.astype(jnp.bfloat16)


def grad_blocks(side, line, normed, grad_expanded, grad_out, product, received=()):
    tokens, width = normed.shape
    rows = width // (2 * line)
    picked = pl.BlockSpec((tokens, rows), lambda q, side_ref: (0, 2 * q + side_ref[0]))
    if rows % LANES:
        picked = pl.BlockSpec((1, tokens, rows), lambda q, side_ref: (2 * q + side_ref[0], 0, 0))
        normed = jnp.transpose(normed.reshape(tokens, 2 * line, rows), (1, 0, 2))
        grad_out = jnp.transpose(grad_out.reshape(tokens, 2 * line, rows), (1, 0, 2))
    wide = [grad_expanded.shape[1], product.shape[1]]
    whole = [pl.BlockSpec((tokens, w), lambda q, side_ref: (0, 0)) for w in wide]
    block = [pl.BlockSpec((1, rows, w), lambda q, side_ref: (q, 0, 0)) for w in wide]
    return pl.pallas_call(
        grad_blocks_kernel,
        grid_spec=pltpu.PrefetchScalarGridSpec(
            num_scalar_prefetch=1,
            grid=(line,),
            in_specs=[picked, whole[0], picked, whole[1]] + block[: len(received)],
            out_specs=block,
        ),
        out_shape=[jax.ShapeDtypeStruct((line, rows, w), jnp.bfloat16) for w in wide],
        cost_estimate=pl.CostEstimate(
            flops=tokens * width * sum(wide), bytes_accessed=6 * tokens * width, transcendentals=0
        ),
        name="grad_blocks",
    )(side, normed, grad_expanded, grad_out, product, *received)


def pick(array, index, axis):
    return lax.dynamic_index_in_dim(array, index, axis, keepdims=False)


def body(
    ctx_size,
    fsdp_size,
    inputs,
    segment_ids,
    gain_attn,
    w_qkv,
    w_out_attn,
    gain_mlp,
    w_in,
    w_out_mlp,
    cotangent,
):
    tok_count, width = inputs.shape[1:]
    heads = HEADS
    head_size = HD
    scale = 1.0 / math.sqrt(head_size)
    hidden_units = w_out_mlp.shape[0]
    row_count = ctx_size * tok_count
    own_heads = heads // ctx_size
    own_width = own_heads * head_size
    weight_rows = w_qkv.shape[0]
    own_hidden = hidden_units // fsdp_size
    own_out = width // fsdp_size
    line = ctx_size // 2
    block_rows = width // ctx_size
    sizes = (ctx_size, fsdp_size)
    bf16 = jnp.bfloat16
    f32 = jnp.float32
    ctx_index = lax.axis_index("ctx")
    parity = ctx_index % 2
    pos = ctx_index // 2

    qkv_parts = jnp.transpose(
        w_qkv.reshape(weight_rows, 3, ctx_size, own_width), (2, 0, 1, 3)
    ).reshape(ctx_size, weight_rows, 3 * own_width)
    gains_own = jnp.pad(jnp.stack([gain_attn, gain_mlp], axis=1), ((0, 0), (0, LANES - 2)))
    qkv_parts = jnp.concatenate(
        [qkv_parts, jnp.broadcast_to(gains_own, (ctx_size, weight_rows, LANES))], axis=2
    )
    in_parts = jnp.transpose(
        w_in.reshape(weight_rows, 2, fsdp_size, own_hidden), (2, 0, 1, 3)
    ).reshape(fsdp_size, weight_rows, 2 * own_hidden)
    mlp_parts = jnp.transpose(w_out_mlp.reshape(fsdp_size, own_hidden, weight_rows), (0, 2, 1))
    seg_own = jnp.broadcast_to(segment_ids.astype(f32), (8, tok_count))

    tokens_all, seg_all, qkv_all, out_all, in_all, mlp_all, grad_out_group = gather_all(
        sizes, inputs[0], seg_own, qkv_parts, w_out_attn, in_parts, mlp_parts, cotangent[0]
    )
    qkv_got = qkv_all.reshape(width, 3 * own_width + LANES)
    qkv_mine = qkv_got[:, : 3 * own_width]
    gains = qkv_got[:, 3 * own_width : 3 * own_width + 2].astype(f32).T
    gain_first = gains[0]
    gain_second = gains[1]
    attn_full = out_all.reshape(width, width)
    in_mine = in_all.reshape(width, 2 * own_hidden)
    mlp_turned = mlp_all.reshape(width, own_hidden)

    seg_row = seg_all[:, 0].reshape(1, row_count)
    seg_col = seg_row.reshape(row_count, 1)
    row_tokens = tokens_all.reshape(row_count, width).astype(f32)
    row_normed, unused = layer_norm(row_tokens)
    row_normed_attn = (row_normed * gain_first).astype(bf16)
    tokens = inputs[0].astype(f32)
    normed_one, scale_one = layer_norm(tokens)

    projected_cols = jnp.einsum(
        "de,td->et", qkv_mine, row_normed_attn, preferred_element_type=f32
    ).reshape(3, own_heads, head_size, row_count)
    positions = jnp.arange(row_count, dtype=jnp.int32).astype(f32)
    cosine, sine = rope_columns(positions, head_size)
    query_cols = rotate_cols(projected_cols[0], cosine, sine).astype(bf16)
    key_cols = rotate_cols(projected_cols[1], cosine, sine).astype(bf16)
    value_cols = projected_cols[2].astype(bf16)
    row_attended, log_total = attend(query_cols, key_cols, value_cols, seg_col, seg_row, scale)

    (attended,) = stage(
        "swap_attended",
        2,
        sizes,
        ("ctx",),
        (row_attended.reshape(own_width, row_count).T.reshape(ctx_size, tok_count, own_width),),
    )
    attended = jnp.transpose(attended, (1, 0, 2)).reshape(tok_count, width)
    residual = tokens + jnp.dot(attended, attn_full, preferred_element_type=f32)
    normed_two, scale_two = layer_norm(residual)
    normed_mlp = (normed_two * gain_second).astype(bf16)
    (normed_group,) = stage("gather_normed", 3, sizes, ("gather",), (normed_mlp,))
    group = fsdp_size * tok_count
    normed_group = normed_group.reshape(group, width)
    grad_out_group = grad_out_group.reshape(group, width)

    expanded = jnp.dot(normed_group, in_mine, preferred_element_type=f32)
    pre_act = expanded[:, :own_hidden]
    gate_part = expanded[:, own_hidden:]
    activated = jax.nn.gelu(pre_act, approximate=False)
    product = (activated * gate_part).astype(bf16)
    grad_product = jnp.einsum("td,df->tf", grad_out_group, mlp_turned, preferred_element_type=f32)
    grad_expanded = jnp.concatenate(
        [grad_product * gate_part * gelu_slope(pre_act), grad_product * activated], axis=1
    ).astype(bf16)
    grad_normed_part = jnp.einsum(
        "tf,df->td", grad_expanded, in_mine, preferred_element_type=f32
    ).astype(bf16)
    out_part = jnp.einsum("tf,df->td", product, mlp_turned, preferred_element_type=f32).astype(bf16)

    (grad_normed_parts,) = stage(
        "swap_grad_normed",
        4,
        sizes,
        ("fsdp",),
        (grad_normed_part.reshape(fsdp_size, tok_count, width),),
    )
    grad_normed_mlp = jnp.sum(grad_normed_parts.astype(f32), axis=0)

    side = jnp.reshape(parity, (1,)).astype(jnp.int32)
    swap_pair = [(i, i ^ 1) for i in range(ctx_size)]
    sent = grad_blocks(1 - side, line, normed_group, grad_expanded, grad_out_group, product)
    received = [lax.ppermute(blocks, "ctx", swap_pair) for blocks in sent]

    grad_gain_two = jnp.sum(grad_normed_mlp * normed_two, axis=0)
    grad_residual = cotangent[0].astype(f32) + norm_back(
        grad_normed_mlp * gain_second, normed_two, scale_two
    )
    residual_half = grad_residual.astype(bf16)
    grad_attended = jnp.einsum(
        "te,de->td", residual_half, attn_full, preferred_element_type=f32
    ).astype(bf16)
    row_grad, residual_cols, attended_group = stage(
        "swap_grad_attended",
        5,
        sizes,
        ("ctx", "fsdp", "gather"),
        (
            jnp.transpose(grad_attended.reshape(tok_count, ctx_size, own_width), (1, 0, 2)),
            jnp.transpose(residual_half.reshape(tok_count, fsdp_size, own_out), (1, 0, 2)),
            attended,
        ),
    )
    grad_attn_part = jnp.einsum(
        "td,te->de",
        attended_group.reshape(group, width),
        residual_cols.reshape(group, own_out),
        preferred_element_type=f32,
    ).reshape(line, 2, block_rows, own_out)
    row_grad_cols = row_grad.reshape(row_count, own_width).T.reshape(
        own_heads, head_size, row_count
    )
    grad_query, grad_key, grad_value = attend_grads(
        query_cols,
        key_cols,
        value_cols,
        seg_col,
        seg_row,
        log_total,
        row_grad_cols,
        row_attended,
        scale,
    )
    grad_proj_cols = (
        jnp.stack(
            [
                unrotate_cols(grad_query, cosine, sine),
                unrotate_cols(grad_key, cosine, sine),
                grad_value,
            ],
            axis=0,
        )
        .astype(bf16)
        .reshape(3 * own_width, row_count)
    )
    row_grad_normed = jnp.einsum("de,et->td", qkv_mine, grad_proj_cols, preferred_element_type=f32)
    grad_gain_part = jnp.sum(row_grad_normed * row_normed, axis=0)
    gain_columns = jnp.pad(
        jnp.stack([grad_gain_part, grad_gain_two], axis=1), ((0, 0), (0, LANES - 2))
    )
    qkv_terms = jnp.concatenate(
        [
            jnp.einsum("td,et->de", row_normed_attn, grad_proj_cols, preferred_element_type=f32),
            gain_columns,
        ],
        axis=1,
    ).astype(bf16)
    qkv_width = 3 * own_width + LANES
    qkv_terms = jnp.transpose(
        qkv_terms.reshape(ctx_size, fsdp_size, weight_rows, qkv_width), (1, 0, 2, 3)
    )
    row_grad_blocks = row_grad_normed.reshape(line, 2, tok_count, width)
    row_grad_half = row_grad_blocks.astype(bf16)
    grad_attn_half = grad_attn_part.astype(bf16)
    in_sum, mlp_sum = grad_blocks(
        side, line, normed_group, grad_expanded, grad_out_group, product, received
    )
    row_other, attn_other, in_lines, mlp_lines, qkv_got_terms, out_parts = stage(
        "pair_stage",
        6,
        sizes,
        ("pair", "pair", "line", "line", "fsdp", "fsdp"),
        (
            row_grad_half,
            grad_attn_half,
            in_sum,
            mlp_sum,
            qkv_terms,
            out_part.reshape(fsdp_size, tok_count, width),
        ),
    )
    block_out = (residual + jnp.sum(out_parts.astype(f32), axis=0)).astype(bf16)
    row_sum = (pick(row_grad_half, parity, 1).astype(f32) + row_other.astype(f32)).astype(bf16)
    attn_sum = (pick(grad_attn_half, parity, 1).astype(f32) + attn_other.astype(f32)).astype(bf16)
    qkv_half = jnp.sum(qkv_got_terms.astype(f32), axis=0).astype(bf16)
    grad_in_block = jnp.sum(in_lines.astype(f32), axis=0).astype(bf16)
    grad_mlp_block = jnp.sum(mlp_lines.astype(f32), axis=0).astype(bf16)
    row_lines, attn_lines, qkv_lines, in_got, mlp_got = stage(
        "line_stage",
        7,
        sizes,
        ("line", "line", "ctx", "fsdp", "fsdp"),
        (
            row_sum,
            attn_sum,
            qkv_half,
            grad_in_block.reshape(fsdp_size, weight_rows, 2 * own_hidden),
            grad_mlp_block.reshape(fsdp_size, weight_rows, own_hidden),
        ),
    )
    grad_normed_attn = jnp.sum(row_lines.astype(f32), axis=0)
    grad_attn_block = jnp.sum(attn_lines.astype(f32), axis=0).astype(bf16)
    grad_tokens = (
        grad_residual + norm_back(grad_normed_attn * gain_first, normed_one, scale_one)
    ).astype(bf16)
    grad_qkv_rows = jnp.transpose(
        qkv_lines[:, :, : 3 * own_width].astype(f32).reshape(ctx_size, weight_rows, 3, own_width),
        (1, 2, 0, 3),
    ).reshape(weight_rows, 3 * width)
    gain_sums = jnp.sum(qkv_lines[:, :, 3 * own_width : 3 * own_width + 2].astype(f32), axis=0)

    (attn_got,) = stage(
        "swap_weight_grads",
        8,
        sizes,
        ("fsdp",),
        (grad_attn_block.reshape(fsdp_size, weight_rows, own_out),),
    )
    grad_in_rows = jnp.transpose(
        in_got.astype(f32).reshape(fsdp_size, weight_rows, 2, own_hidden), (1, 2, 0, 3)
    ).reshape(weight_rows, 2 * hidden_units)
    grad_mlp_cols = jnp.transpose(mlp_got.astype(f32), (0, 2, 1)).reshape(hidden_units, weight_rows)
    grad_attn_rows = jnp.transpose(attn_got.astype(f32), (1, 0, 2)).reshape(weight_rows, width)
    return (
        block_out[None],
        grad_tokens[None],
        grad_qkv_rows,
        grad_attn_rows,
        grad_in_rows,
        grad_mlp_cols,
        gain_sums[:, 0],
        gain_sums[:, 1],
    )


def solution(mesh):
    in_specs = (
        P("fsdp", "ctx", None),
        P("fsdp", "ctx"),
        P(("ctx", "fsdp")),
        P(("ctx", "fsdp"), None),
        P(("ctx", "fsdp"), None),
        P(("ctx", "fsdp")),
        P(("ctx", "fsdp"), None),
        P(None, ("ctx", "fsdp")),
        P("fsdp", "ctx", None),
    )
    out_specs = (
        P("fsdp", "ctx", None),
        P("fsdp", "ctx", None),
        P(("ctx", "fsdp"), None),
        P(("ctx", "fsdp"), None),
        P(("ctx", "fsdp"), None),
        P(None, ("ctx", "fsdp")),
        P(("ctx", "fsdp")),
        P(("ctx", "fsdp")),
    )
    step = functools.partial(body, mesh.shape["ctx"], mesh.shape["fsdp"])
    return jax.shard_map(step, mesh=mesh, in_specs=in_specs, out_specs=out_specs, check_vma=False)
```
